1024 devices in a mesh: lat: 32 (over x_hi, z), lon: 32 (over y, x_lo, core).
Axes of the slice: x: 4 (x_hi: 2, x_lo: 2; x = x_hi * 2 + x_lo), y: 8, z: 16, core: 2. Of those that a mesh axis runs over, the one named last changes fastest.
Arguments:
- coarse: bfloat16 [2, 192, 192, 1024], P(None, 'lat', 'lon'), may hold values from -6 to 6
- skip_tokens: bfloat16 [2, 384, 384, 512], P(None, 'lat', 'lon'), may hold values from -40 to 40
- land_sea: int32 [384, 384], P('lat', 'lon'), may hold values from 0 to 2
- surf_table: float32 [3, 512], replicated, may hold values from -5 to 5
- expand_weight: bfloat16 [1024, 2048], replicated, may hold values from -0.1875 to 0.1875
- expand_gain: float32 [512], replicated, may hold values from 0.1 to 1.9
- attn_gain: float32 [512], replicated, may hold values from 0.1 to 1.9
- qkv_weight: bfloat16 [512, 1536], replicated, may hold values from -0.25 to 0.25
- logit_scale: float32 [8], replicated, may hold values from 2 to 20
- out_weight: bfloat16 [512, 512], replicated, may hold values from -0.25 to 0.25
Outputs:
- mixed: float32 [2, 384, 384, 512], P(None, 'lat', 'lon')
The draws below stay inside these ranges and needn't reach their ends.
All inputs are finite; a program needn't handle non-finite values.
Results may differ from the reference program's by a relative error of at most 0.003.
Values may be sent and summed in bfloat16 or wider, within the bound.
No kernel may reach another device: no remote copies, remote signals or barrier semaphores. Data moves between devices by JAX's collectives and lax.ppermute only.
A program may use at most 32 MiB of HBM per device.

```python
import math
import jax
import jax.numpy as jnp
from jax import lax

D = 512
CD = 1024
HEADS = 8
CLASSES = 3
Z = 2
WIN_LAT = 6
WIN_LON = 12
SHIFT_LAT = 3
SHIFT_LON = 6
H2 = 192
W2 = 192
H = 384
W = 384


def draw_skip_tokens(key, part):
    key_values, key_rows, key_columns = jax.random.split(key, 3)
    row_scale = jnp.exp(jax.random.uniform(key_rows, (Z, H, W, 1), jnp.float32, jnp.log(0.3), jnp.log(3.0)))
    column_scale = jnp.exp(jax.random.uniform(key_columns, (1, 1, 1, D), jnp.float32, jnp.log(0.3), jnp.log(3.0)))
    values = jnp.clip(jax.random.normal(key_values, (Z, H, W, D), jnp.float32), -4.0, 4.0)
    return (values * row_scale * column_scale).astype(jnp.bfloat16)


def plant(values, key, low, largest):
    longest = values.shape.index(max(values.shape))
    spots = []
    for shift in (0, 1):
        where = [jax.random.randint(jax.random.fold_in(key, axis), (), 0, length) for axis, length in enumerate(values.shape)]
        where[longest] = (where[longest] + shift) % values.shape[longest]
        spots.append(tuple(where))
    return values.at[spots[0]].set(low).at[spots[1]].set(largest)


def block_scale(stream_key, extent, cuts, smallest, high):
    level = 1.0
    for axis_at, blocks in cuts:
        heights = jax.random.uniform(jax.random.fold_in(jax.random.fold_in(stream_key, 6), axis_at), (blocks,), jnp.float32, smallest / len(cuts), high / len(cuts))
        level = level * jnp.repeat(jnp.exp(heights), extent[axis_at] // blocks).reshape((-1,) + (1,) * (len(extent) - 1 - axis_at))
    return level


def gaussian(stream_key, shape, deviation, reach, pieces=(), kind=jnp.bfloat16):
    loudness = block_scale(stream_key, shape, pieces, -0.22, 0.18) if pieces else 1.0
    entries = jax.random.normal(stream_key, shape, jnp.float32) * deviation * loudness
    return jnp.minimum(jnp.maximum(entries, -reach), reach).astype(kind)


def setup_inputs(seed: int = 0) -> dict:
    seeds = jax.random.split(jax.random.key(seed), 11)
    coarse = gaussian(seeds[0], (Z, H2, W2, CD), 1.0, 6.0, ((1, 32), (2, 32)))
    skip_tokens = draw_skip_tokens(jax.random.fold_in(seeds[10], 71), 0)
    land_sea = plant(jax.random.randint(seeds[2], (H, W), 0, CLASSES), jax.random.fold_in(seeds[2], 1), 0, CLASSES - 1).astype(jnp.int32)
    surf_table = gaussian(seeds[3], (CLASSES, D), 1.0, 5.0, (), jnp.float32)
    expand_weight = gaussian(seeds[4], (CD, 4 * D), CD ** -0.5, 0.1875)
    expand_gain = jnp.clip(1.0 + 0.18 * jax.random.normal(seeds[5], (D,), jnp.float32), 0.1, 1.9)
    attn_gain = jnp.clip(1.0 + 0.18 * jax.random.normal(seeds[6], (D,), jnp.float32), 0.1, 1.9)
    qkv_weight = gaussian(seeds[7], (D, 3 * D), D ** -0.5, 0.25)
    logit_scale = jnp.clip(jnp.exp(jax.random.uniform(seeds[8], (HEADS,), jnp.float32, math.log(2.0), math.log(20.0))), 2.0, 20.0)
    out_weight = gaussian(seeds[9], (D, D), D ** -0.5, 0.25)
    return dict(coarse=coarse, skip_tokens=skip_tokens, land_sea=land_sea, surf_table=surf_table, expand_weight=expand_weight, expand_gain=expand_gain, attn_gain=attn_gain, qkv_weight=qkv_weight, logit_scale=logit_scale, out_weight=out_weight)


EPSILON = 1e-05

def layer_norm(values, gain_vector):
    average = lax.optimization_barrier(jnp.mean(values, axis=-1, keepdims=True))
    centred = values - average
    spread = lax.optimization_barrier(jnp.mean(centred * centred, axis=-1, keepdims=True))
    return centred * lax.rsqrt(spread + EPSILON) * gain_vector

def expand_tokens(coarse, expand_weight, expand_gain):
    levels, height, breadth, channels = coarse.shape
    expanded = jnp.dot(coarse.reshape(-1, channels), expand_weight, preferred_element_type=jnp.float32)
    expanded = expanded.reshape(levels, height, breadth, 2, 2, -1)
    expanded = jnp.transpose(expanded, (0, 1, 3, 2, 4, 5))
    expanded = expanded.reshape(levels, 2 * height, 2 * breadth, -1)
    return layer_norm(expanded, expand_gain)

def surface_terms(land_sea, surf_table):
    result = jnp.zeros(land_sea.shape + (surf_table.shape[1],), jnp.float32)
    for category in range(surf_table.shape[0]):
        picked = (land_sea == category).astype(jnp.float32)
        result = result + picked[:, :, None] * surf_table[category]
    return result

def window_attention(region, row_group, attn_gain, qkv_weight, logit_scale):
    levels, height, breadth, channels = region.shape
    head_count = logit_scale.shape[0]
    head_width = channels // head_count
    lat_windows = height // WIN_LAT
    lon_windows = breadth // WIN_LON
    window_size = levels * WIN_LAT * WIN_LON
    normed = layer_norm(region.astype(jnp.float32), attn_gain).astype(jnp.bfloat16)
    packed = jnp.dot(normed.reshape(-1, channels), qkv_weight, preferred_element_type=jnp.float32).astype(jnp.bfloat16)
    packed = packed.reshape(levels, lat_windows, WIN_LAT, lon_windows, WIN_LON, 3, head_count, head_width)
    packed = jnp.transpose(packed, (5, 1, 3, 6, 0, 2, 4, 7)).reshape(3, lat_windows, lon_windows, head_count, window_size, head_width)
    queries = packed[0].astype(jnp.float32)
    key_rows = packed[1].astype(jnp.float32)
    queries = queries * lax.rsqrt(lax.optimization_barrier(jnp.sum(queries * queries, axis=-1, keepdims=True)) + 1e-06)
    key_rows = key_rows * lax.rsqrt(lax.optimization_barrier(jnp.sum(key_rows * key_rows, axis=-1, keepdims=True)) + 1e-06)
    scores = jnp.einsum('abhqe,abhke->abhqk', queries, key_rows, precision=lax.Precision.HIGHEST)
    scores = scores * logit_scale[None, None, :, None, None]
    token_group = jnp.broadcast_to(row_group.reshape(1, lat_windows, WIN_LAT, 1), (levels, lat_windows, WIN_LAT, WIN_LON))
    token_group = jnp.transpose(token_group, (1, 0, 2, 3)).reshape(lat_windows, window_size)
    allowed = token_group[:, :, None] == token_group[:, None, :]
    weights = jnp.where(allowed[:, None, None], jnp.exp(scores), jnp.float32(0.0))
    attention = (weights / lax.optimization_barrier(jnp.sum(weights, axis=-1, keepdims=True))).astype(jnp.bfloat16)
    blended = jnp.einsum('abhqk,abhke->abhqe', attention.astype(jnp.float32), packed[2].astype(jnp.float32), precision=lax.Precision.HIGHEST).astype(jnp.bfloat16)
    blended = blended.reshape(lat_windows, lon_windows, head_count, levels, WIN_LAT, WIN_LON, head_width)
    blended = jnp.transpose(blended, (3, 0, 4, 1, 5, 2, 6)).reshape(levels, height, breadth, channels)
    return blended

def project(blended, out_weight):
    projected = jnp.dot(blended.reshape(-1, blended.shape[-1]), out_weight, preferred_element_type=jnp.float32)
    return projected.reshape(blended.shape)

def reference(coarse, skip_tokens, land_sea, surf_table, expand_weight, expand_gain, attn_gain, qkv_weight, logit_scale, out_weight):
    fine = expand_tokens(coarse, expand_weight, expand_gain)
    tokens = (skip_tokens.astype(jnp.float32) + fine + surface_terms(land_sea, surf_table)[None]).astype(jnp.bfloat16)
    rolled = jnp.roll(tokens, (-SHIFT_LAT, -SHIFT_LON), axis=(1, 2))
    global_rows = (jnp.arange(H, dtype=jnp.int32) + SHIFT_LAT) % H
    row_group = (global_rows - SHIFT_LAT) // WIN_LAT
    bands = jnp.transpose(rolled.reshape(Z, H // WIN_LAT, WIN_LAT, W, D), (1, 0, 2, 3, 4))
    band_groups = row_group.reshape(H // WIN_LAT, WIN_LAT)

    def one_band(band_pair):
        return window_attention(band_pair[0], band_pair[1], attn_gain, qkv_weight, logit_scale)
    blended = lax.map(one_band, (bands, band_groups))
    blended = jnp.transpose(blended, (1, 0, 2, 3, 4)).reshape(Z, H, W, D)
    blended = jnp.roll(blended, (SHIFT_LAT, SHIFT_LON), axis=(1, 2))
    return tokens.astype(jnp.float32) + project(blended, out_weight)
```

```python
import functools

import jax
import jax.numpy as jnp
import numpy as np
from jax import lax
from jax.experimental import pallas as pl
from jax.experimental.pallas import tpu as pltpu
from jax.sharding import PartitionSpec as P

D = 512
HEADS = 8
HEAD = 64
ROWS = 12
COLS = 12
Z = 2
EPSILON = 1e-05

HALF = 152
MID, EDGE, EDGE_LIVE = 72, 40, 36
OWN = 2 * HALF


def half_tokens(half):
    columns = range(6 * half, 6 * half + 6)
    listed = []
    for rows, size in ((range(3, 9), MID), (range(0, 3), EDGE), (range(9, 12), EDGE)):
        part = [(r, c, z) for r in rows for c in columns for z in range(Z)]
        listed += part + [None] * (size - len(part))
    return listed


KEPT = half_tokens(0) + half_tokens(1)


def natural(r, c, z):
    return (r * COLS + c) * Z + z


def selections():
    to_phase = np.zeros((4, 72, 288), np.float32)
    to_kept = np.zeros((4, OWN, 72), np.float32)
    to_natural = np.zeros((288, OWN), np.float32)
    for r in range(ROWS):
        for c in range(COLS):
            for z in range(Z):
                phase = 2 * (r % 2) + c % 2
                place = ((r // 2) * 6 + c // 2) * Z + z
                to_phase[phase, place, natural(r, c, z)] = 1.0
                kept = KEPT.index((r, c, z))
                to_kept[phase, kept, place] = 1.0
                to_natural[natural(r, c, z), kept] = 1.0
    return to_phase, to_kept, to_natural


TO_PHASE, TO_KEPT, TO_NATURAL = selections()


def normalized(values, gain):
    average = jnp.mean(values, axis=-1, keepdims=True)
    centred = values - average
    spread = jnp.mean(centred * centred, axis=-1, keepdims=True)
    return centred * lax.rsqrt(spread + EPSILON) * gain


def dot(a, b):
    return jnp.dot(a, b, preferred_element_type=jnp.float32)


def expand_kernel(coarse, weight, skip, surface, table, gain, to_phase, to_kept, out, total):
    phase = pl.program_id(0)
    fine = normalized(dot(coarse[...], weight[...]), gain[...])
    beside = dot(to_phase[0], skip[...])
    kind = surface[0]
    term = jnp.where(kind == 0, table[0:1], jnp.where(kind == 1, table[1:2], table[2:3]))
    tokens = (beside + fine + term).astype(jnp.bfloat16)
    placed = dot(to_kept[0], tokens)

    @pl.when(phase == 0)
    def _():
        total[...] = placed

    @pl.when(phase > 0)
    def _():
        total[...] += placed

    @pl.when(phase == 3)
    def _():
        out[...] = total[...].astype(jnp.bfloat16)


def expand(coarse, skip, land_sea, surf_table, expand_weight, expand_gain):
    rows = jnp.transpose(coarse, (1, 2, 0, 3)).reshape(72, 1024)
    beside = jnp.transpose(skip, (1, 2, 0, 3)).reshape(288, D)
    kinds = jnp.transpose(land_sea.reshape(6, 2, 6, 2), (1, 3, 0, 2)).reshape(4, 36, 1)
    kinds = jnp.broadcast_to(kinds, (4, 36, 2)).reshape(4, 72, 1)
    whole = lambda shape: pl.BlockSpec(shape, lambda i: (0,) * len(shape))
    return pl.pallas_call(
        expand_kernel,
        grid=(4,),
        out_shape=jax.ShapeDtypeStruct((OWN, D), jnp.bfloat16),
        in_specs=[
            whole((72, 1024)),
            pl.BlockSpec((1024, D), lambda i: (0, i)),
            whole((288, D)),
            pl.BlockSpec((1, 72, 1), lambda i: (i, 0, 0)),
            whole((3, D)),
            whole((1, D)),
            pl.BlockSpec((1, 72, 288), lambda i: (i, 0, 0)),
            pl.BlockSpec((1, OWN, 72), lambda i: (i, 0, 0)),
        ],
        out_specs=whole((OWN, D)),
        scratch_shapes=[pltpu.VMEM((OWN, D), jnp.float32)],
        cost_estimate=pl.CostEstimate(flops=2 * 72 * 1024 * 2048, bytes_accessed=5 << 20, transcendentals=0),
        name="expand",
    )(
        rows,
        expand_weight,
        beside,
        kinds,
        surf_table,
        expand_gain.reshape(1, D),
        jnp.asarray(TO_PHASE, jnp.bfloat16),
        jnp.asarray(TO_KEPT, jnp.bfloat16),
    )


PARTS = ((0, MID), (MID, EDGE), (MID + EDGE, EDGE))


def attention_kernel(
    own, left, right, above, below, gain, weight, scale, ones, out_weight, to_natural, out, blended
):
    lat = lax.axis_index("lat")
    last = lax.axis_size("lat") - 1
    bf16 = lambda v: v.astype(jnp.bfloat16)
    pieces, starts, asked = [], [], []
    for half, beside in ((0, left), (1, right)):
        for part, (first, size) in enumerate(PARTS):
            starts.append(sum(p.shape[0] for p in pieces))
            mine = own[half * HALF + first : half * HALF + first + size].astype(jnp.float32)
            window = [mine, beside[first : first + size].astype(jnp.float32)]
            if part:
                outside = above if part == 1 else below
                for side in (0, 1):
                    at = (2 * half + side) * EDGE
                    window.append(outside[at : at + EDGE].astype(jnp.float32))
            window = jnp.concatenate(window, axis=0)
            window = normalized(window, gain[...])
            pieces.append(window)
            asked.append(window[:size])
    every = bf16(jnp.concatenate(pieces, axis=0))
    asking = bf16(jnp.concatenate(asked, axis=0))
    lane = lax.broadcasted_iota(jnp.int32, (1, 256), 1) // HEAD
    for group in (0, 1):
        at = group * 256

        def unit(rows, column, factor):
            product = bf16(dot(rows, weight[:, column : column + 256])).astype(jnp.float32)
            squares = dot(bf16(product * product), ones[...])
            product = product * lax.rsqrt(squares + 1e-06)
            return product if factor is None else product * factor

        queries = unit(asking, at, scale[:, at : at + 256])
        keys = bf16(unit(every, D + at, None))
        values = bf16(dot(every, weight[:, 2 * D + at : 2 * D + at + 256]))
        q_at = 0
        for window in range(6):
            part = window % 3
            size = PARTS[part][1]
            count = 144 if part == 0 else 4 * EDGE
            first = starts[window]
            k = keys[first : first + count]
            v = values[first : first + count]
            q = queries[q_at : q_at + size]
            stacked = bf16(jnp.concatenate([jnp.where(lane == h, q, 0.0) for h in range(4)], axis=0))
            scores = lax.dot_general(stacked, k, (((1,), (1,)), ((), ())), preferred_element_type=jnp.float32)
            powers = jnp.exp(scores)
            if part:
                key = lax.broadcasted_iota(jnp.int32, (1, count), 1)
                inside = lat > 0 if part == 1 else lat < last
                limit = jnp.where(inside, count, 2 * EDGE)
                live = (lax.rem(key, EDGE) < EDGE_LIVE) & (key < limit)
                powers = jnp.where(live, powers, 0.0)
            share = 1.0 / jnp.sum(powers, axis=-1, keepdims=True)
            mixed = dot(bf16(powers), v) * share
            result = jnp.where(lane == 0, mixed[:size], 0.0)
            for h in range(1, 4):
                result = jnp.where(lane == h, mixed[h * size : (h + 1) * size], result)
            blended[q_at : q_at + size, at : at + 256] = result
            q_at += size
    placed = bf16(dot(to_natural[...], bf16(blended[...])))
    tokens = dot(to_natural[...], own[...])
    out[...] = tokens + dot(placed, out_weight[...])


def attention(own, left, right, above, below, attn_gain, qkv_weight, logit_scale, out_weight):
    ones = np.kron(np.eye(4, dtype=np.float32), np.ones((HEAD, HEAD), np.float32))
    return pl.pallas_call(
        attention_kernel,
        out_shape=jax.ShapeDtypeStruct((288, D), jnp.float32),
        in_specs=[pl.BlockSpec(memory_space=pltpu.VMEM)] * 11,
        out_specs=pl.BlockSpec(memory_space=pltpu.VMEM),
        scratch_shapes=[pltpu.VMEM((OWN, D), jnp.float32)],
        cost_estimate=pl.CostEstimate(flops=4 << 30, bytes_accessed=4 << 20, transcendentals=700000),
        name="attention",
    )(
        own,
        left,
        right,
        above,
        below,
        attn_gain.reshape(1, D),
        qkv_weight,
        jnp.repeat(logit_scale, HEAD).reshape(1, D),
        jnp.asarray(ones, jnp.bfloat16),
        out_weight,
        jnp.asarray(TO_NATURAL, jnp.bfloat16),
    )


def shifted(value, axis, steps, wrap):
    count = lax.axis_size(axis)
    pairs = [(source, (source + steps) % count) for source in range(count) if wrap or 0 <= source + steps < count]
    return lax.ppermute(value, axis, pairs)


def per_device(
    coarse,
    skip_tokens,
    land_sea,
    surf_table,
    expand_weight,
    expand_gain,
    attn_gain,
    qkv_weight,
    logit_scale,
    out_weight,
):
    own = expand(coarse, skip_tokens, land_sea, surf_table, expand_weight, expand_gain)
    right = shifted(own[:HALF], "lon", -1, True)
    left = shifted(own[HALF:], "lon", 1, True)
    parts = (own[:HALF], left, own[HALF:], right)
    top = jnp.concatenate([p[MID : MID + EDGE] for p in parts], axis=0)
    bottom = jnp.concatenate([p[MID + EDGE :] for p in parts], axis=0)
    below = shifted(top, "lat", -1, False)
    above = shifted(bottom, "lat", 1, False)
    mixed = attention(own, left, right, above, below, attn_gain, qkv_weight, logit_scale, out_weight)
    return jnp.transpose(mixed.reshape(ROWS, COLS, Z, D), (2, 0, 1, 3))


def solution(mesh):
    in_specs = (
        P(None, "lat", "lon", None),
        P(None, "lat", "lon", None),
        P("lat", "lon"),
        P(),
        P(),
        P(),
        P(),
        P(),
        P(),
        P(),
    )
    out_specs = P(None, "lat", "lon", None)
    return jax.shard_map(
        per_device, mesh=mesh, in_specs=in_specs, out_specs=out_specs, check_vma=False
    )
```

```python
import jax
import jax.numpy as jnp
from jax import lax
from jax.experimental import pallas as pl
from jax.experimental.pallas import tpu as pltpu
from jax.sharding import PartitionSpec as P

D = 512
CD = 1024
HEAD = 64
ROWS = 12
COLS = 12
HALF = 6
EDGE = 3
Z = 2
EPSILON = 1e-05
MIB = 1 << 20


def half_start(half, position):
    return HALF * ((half + position + 1) % 2)


def edge_start(edge, position):
    return (ROWS - EDGE) * ((edge + position + 1) % 2)


def flat(tokens):
    return tokens.reshape(-1, tokens.shape[-1])


def normalized(values, gain):
    average = jnp.mean(values, axis=-1, keepdims=True)
    centred = values - average
    spread = jnp.mean(centred * centred, axis=-1, keepdims=True)
    return centred * lax.rsqrt(spread + EPSILON) * gain


def dot(a, b):
    return jnp.dot(a, b, preferred_element_type=jnp.float32)


def expand_kernel(coarse, weight, skip, surface, table, gain, half0, half1, *scratch):
    even = lax.rem(lax.axis_index("lon"), 2) == 0
    buffer, coarse_in, skip_in, surface_in, table_in, gain_in, arrived = scratch
    small = [
        pltpu.make_async_copy(source, target, arrived.at[4 + at])
        for at, (source, target) in enumerate(
            ((coarse, coarse_in), (surface, surface_in), (table, table_in), (gain, gain_in), (skip, skip_in))
        )
    ]
    large = [
        pltpu.make_async_copy(weight.at[:, phase * D : (phase + 1) * D], buffer.at[phase], arrived.at[phase])
        for phase in range(4)
    ]
    for copy in small + large:
        copy.start()
    place = lax.broadcasted_iota(jnp.int32, (72, ROWS), 0)
    lane = lax.broadcasted_iota(jnp.int32, (72, ROWS), 1)
    for copy in small:
        copy.wait()
    rows = flat(coarse_in[...])
    kinds = surface_in[...].astype(jnp.float32)
    added = []
    for phase in range(4):
        a, b = phase // 2, phase % 2
        row_is = (2 * (place // 12) + a == lane).astype(jnp.float32)
        column_is = 2 * (lax.rem(place, 12) // 2) + b == lane
        kind = jnp.sum(jnp.where(column_is, dot(row_is, kinds), 0.0), axis=-1, keepdims=True)
        term = jnp.where(kind == 0, table_in[0:1], jnp.where(kind == 1, table_in[1:2], table_in[2:3]))
        added.append(flat(skip_in[:, a, :, b]).astype(jnp.float32) + term)
    for phase in range(4):
        a, b = phase // 2, phase % 2
        large[phase].wait()
        fine = normalized(dot(rows, buffer[phase]), gain_in[...])
        made = (added[phase] + fine).reshape(6, 6, Z, D)
        first, second = made[:, :3], made[:, 3:]
        half0[:, a, :, b] = jnp.where(even, second, first).astype(jnp.bfloat16)
        half1[:, a, :, b] = jnp.where(even, first, second).astype(jnp.bfloat16)


VMEM = pl.BlockSpec(memory_space=pltpu.VMEM)
HBM = pl.BlockSpec(memory_space=pltpu.HBM)
SMEM = pl.BlockSpec(memory_space=pltpu.SMEM)


def expand(coarse, skip, land_sea, surf_table, expand_weight, expand_gain):
    half = jax.ShapeDtypeStruct((6, 2, 3, 2, Z, D), jnp.bfloat16)
    halves = pl.pallas_call(
        expand_kernel,
        out_shape=(half, half),
        in_specs=[HBM] * 6,
        out_specs=(VMEM, VMEM),
        scratch_shapes=[
            pltpu.VMEM((4, CD, D), jnp.bfloat16),
            pltpu.VMEM((6, 6, Z, CD), jnp.bfloat16),
            pltpu.VMEM((6, 2, 6, 2, Z, D), jnp.bfloat16),
            pltpu.VMEM((ROWS, COLS), jnp.int32),
            pltpu.VMEM((3, D), jnp.float32),
            pltpu.VMEM((1, D), jnp.float32),
            pltpu.SemaphoreType.DMA((9,)),
        ],
        compiler_params=pltpu.CompilerParams(vmem_limit_bytes=16 * MIB),
        cost_estimate=pl.CostEstimate(flops=2 * 72 * CD * 2048, bytes_accessed=5 * MIB, transcendentals=0),
        name="expand",
    )(
        *(
            pltpu.with_memory_space_constraint(operand, pltpu.HBM)
            for operand in (
                jnp.transpose(coarse, (1, 2, 0, 3)),
                expand_weight,
                jnp.transpose(skip, (1, 2, 0, 3)).reshape(6, 2, 6, 2, Z, D),
                land_sea,
                surf_table,
                expand_gain.reshape(1, D),
            )
        )
    )
    return [part.reshape(ROWS, HALF, Z, D) for part in halves]


def bf16(values):
    return values.astype(jnp.bfloat16)


def head_lanes():
    return lax.broadcasted_iota(jnp.int32, (1, 256), 1) // HEAD


def head_ones():
    return bf16((lax.broadcasted_iota(jnp.int32, (256, 256), 0) // HEAD == head_lanes()).astype(jnp.float32))


def projected(rows, weight, column):
    return bf16(dot(rows, weight[:, column : column + 256]))


def unit(rows, weight, column, ones):
    product = projected(rows, weight, column).astype(jnp.float32)
    squares = dot(bf16(product * product), ones)
    return product * lax.rsqrt(squares + 1e-06)


def scaled_queries(rows, weight, group, scale, ones):
    lane = head_lanes()
    factor = jnp.full((1, 256), scale[4 * group], jnp.float32)
    for h in range(1, 4):
        factor = jnp.where(lane == h, scale[4 * group + h], factor)
    return unit(rows, weight, 256 * group, ones) * factor


def attended(q, keys, values, live=None):
    size = q.shape[0]
    lane = head_lanes()
    stacked = bf16(jnp.concatenate([jnp.where(lane == h, q, 0.0) for h in range(4)], axis=0))
    scores = lax.dot_general(stacked, keys, (((1,), (1,)), ((), ())), preferred_element_type=jnp.float32)
    powers = jnp.exp(scores)
    if live is not None:
        powers = jnp.where(live, powers, 0.0)
    share = 1.0 / jnp.sum(powers, axis=-1, keepdims=True)
    mixed = dot(bf16(powers), values) * share
    result = jnp.where(lane == 0, mixed[:size], 0.0)
    for h in range(1, 4):
        result = jnp.where(lane == h, mixed[h * size : (h + 1) * size], result)
    return bf16(result)


def pairs_of(tokens):
    return tokens.reshape(-1, Z, D)


def middle_kernel(mine0, mine1, beside0, beside1, gain, weight, scale, out_weight, out, made, blended, sent):
    lon = lax.axis_index("lon")
    middle = pl.ds(EDGE, ROWS - 2 * EDGE)
    ones = head_ones()
    tokens = [
        flat(jnp.concatenate([pairs_of(mine[middle]), pairs_of(beside[middle])], axis=0)).astype(jnp.float32)
        for mine, beside in ((mine0, beside0), (mine1, beside1))
    ]
    normed = [normalized(window, gain[...]) for window in tokens]
    every = bf16(jnp.concatenate(normed, axis=0))
    asking = bf16(jnp.concatenate([window[:72] for window in normed], axis=0))
    for group in (0, 1):
        queries = scaled_queries(asking, weight, group, scale, ones)
        keys = bf16(unit(every, weight, D + 256 * group, ones))
        values = projected(every, weight, 2 * D + 256 * group)
        for half in (0, 1):
            window = slice(144 * half, 144 * half + 144)
            blended[72 * half : 72 * half + 72, 256 * group : 256 * group + 256] = attended(
                queries[72 * half : 72 * half + 72], keys[window], values[window]
            )
    result = jnp.concatenate([window[:72] for window in tokens], axis=0) + dot(blended[...], out_weight[...])
    for half in (0, 1):
        made[:, pl.ds(half_start(half, lon), HALF)] = result[72 * half : 72 * half + 72].reshape(6, HALF, Z, D)
    copy = pltpu.make_async_copy(made, out.at[middle], sent)
    copy.start()
    copy.wait()


def edge_kernel(
    mine0, mine1, beside0, beside1, over0, over1, gain, weight, scale, out_weight, begun, out, made, blended, sent
):
    lat, lon = lax.axis_index("lat"), lax.axis_index("lon")
    last = lax.axis_size("lat") - 1
    ones = head_ones()
    tokens = []
    for edge, over in ((0, over0), (1, over1)):
        rows = pl.ds(edge_start(edge, lat), EDGE)
        for half, mine, beside in ((0, mine0, beside0), (1, mine1, beside1)):
            window = [mine[rows], beside[rows], over[2 * half], over[2 * half + 1]]
            window = jnp.concatenate([pairs_of(w) for w in window], axis=0)
            tokens.append(flat(window).astype(jnp.float32))
    normed = [normalized(window, gain[...]) for window in tokens]
    every = bf16(jnp.concatenate(normed, axis=0))
    asking = bf16(jnp.concatenate([window[:40] for window in normed], axis=0))
    paired = jnp.where((lat > 0) & (lat < last), 144, 72)
    live = lax.broadcasted_iota(jnp.int32, (1, 144), 1) < paired
    for group in (0, 1):
        queries = scaled_queries(asking, weight, group, scale, ones)
        keys = bf16(unit(every, weight, D + 256 * group, ones))
        values = projected(every, weight, 2 * D + 256 * group)
        for at in range(4):
            window = slice(144 * at, 144 * at + 144)
            blended[40 * at : 40 * at + 40, 256 * group : 256 * group + 256] = attended(
                queries[40 * at : 40 * at + 40], keys[window], values[window], live if at >= 2 else None
            ).astype(jnp.float32)
    result = jnp.concatenate([window[:40] for window in tokens], axis=0) + dot(bf16(blended[...]), out_weight[...])
    copies = []
    for edge in (0, 1):
        for half in (0, 1):
            at = 40 * (2 * edge + half)
            part = result[at : at + 40].reshape(20, Z, D)[:18].reshape(EDGE, HALF, Z, D)
            made[edge, :, pl.ds(half_start(half, lon), HALF)] = part
        rows = pl.ds(edge_start(edge, lat), EDGE)
        copies.append(pltpu.make_async_copy(made.at[edge], out.at[rows], sent.at[edge]))
    for copy in copies:
        copy.start()
    for copy in copies:
        copy.wait()


OUT = jax.ShapeDtypeStruct((ROWS, COLS, Z, D), jnp.float32)


def middle_windows(mine, beside, parameters):
    return pl.pallas_call(
        middle_kernel,
        out_shape=OUT,
        in_specs=[VMEM] * 6 + [SMEM, VMEM],
        out_specs=HBM,
        scratch_shapes=[
            pltpu.VMEM((6, COLS, Z, D), jnp.float32),
            pltpu.VMEM((144, D), jnp.bfloat16),
            pltpu.SemaphoreType.DMA(()),
        ],
        compiler_params=pltpu.CompilerParams(vmem_limit_bytes=32 * MIB),
        cost_estimate=pl.CostEstimate(flops=2 << 30, bytes_accessed=2 * MIB, transcendentals=350000),
        name="middle",
    )(*mine, *beside, *parameters)


def edge_windows(mine, beside, over, parameters, begun):
    return pl.pallas_call(
        edge_kernel,
        out_shape=OUT,
        in_specs=[VMEM] * 8 + [SMEM, VMEM, HBM],
        out_specs=HBM,
        scratch_shapes=[
            pltpu.VMEM((2, EDGE, COLS, Z, D), jnp.float32),
            pltpu.VMEM((160, D), jnp.float32),
            pltpu.SemaphoreType.DMA((2,)),
        ],
        input_output_aliases={10: 0},
        compiler_params=pltpu.CompilerParams(vmem_limit_bytes=32 * MIB),
        cost_estimate=pl.CostEstimate(flops=2 << 30, bytes_accessed=2 * MIB, transcendentals=350000),
        name="edges",
    )(*mine, *beside, *over, *parameters, begun)


def swapped(value, axis, turn, ring):
    count = lax.axis_size(axis)
    pairs = []
    for source in range(count):
        target = source + 1 if source % 2 == turn else source - 1
        if not ring and not 0 <= target < count:
            target = source
        pairs.append((source, target % count))
    return lax.ppermute(value, axis, pairs)


def per_device(
    coarse,
    skip_tokens,
    land_sea,
    surf_table,
    expand_weight,
    expand_gain,
    attn_gain,
    qkv_weight,
    logit_scale,
    out_weight,
):
    mine = expand(coarse, skip_tokens, land_sea, surf_table, expand_weight, expand_gain)
    beside = [swapped(mine[turn], "lon", turn, True) for turn in (0, 1)]
    lat = lax.axis_index("lat")
    over = [None, None]
    for turn in (1, 0):
        parts = [
            lax.dynamic_slice_in_dim(part, edge_start(turn, lat), EDGE, 0)
            for part in (mine[0], beside[0], mine[1], beside[1])
        ]
        over[turn] = swapped(jnp.stack(parts), "lat", turn, False)
    parameters = (attn_gain.reshape(1, D), qkv_weight, logit_scale, out_weight)
    begun = middle_windows(mine, beside, parameters)
    mixed = edge_windows(mine, beside, over, parameters, begun)
    return jnp.transpose(mixed, (2, 0, 1, 3))


def solution(mesh):
    in_specs = (
        P(None, "lat", "lon", None),
        P(None, "lat", "lon", None),
        P("lat", "lon"),
        P(),
        P(),
        P(),
        P(),
        P(),
        P(),
        P(),
    )
    out_specs = P(None, "lat", "lon", None)
    return jax.shard_map(
        per_device, mesh=mesh, in_specs=in_specs, out_specs=out_specs, check_vma=False
    )
```

```python
import jax
import jax.numpy as jnp
from jax import lax
from jax.experimental import pallas as pl
from jax.experimental.pallas import tpu as pltpu
from jax.sharding import PartitionSpec as P


D = 512
CD = 1024
HEAD = 64
ROWS = 12
COLS = 12
HALF = 6
EDGE = 3
Z = 2
EPSILON = 1e-05
MIB = 1 << 20


def half_start(half, position):
    return HALF * ((half + position + 1) % 2)


def edge_start(edge, position):
    return (ROWS - EDGE) * ((edge + position + 1) % 2)


def flat(tokens):
    return tokens.reshape(-1, tokens.shape[-1])


def normalized(values, gain):
    average = jnp.mean(values, axis=-1, keepdims=True)
    centred = values - average
    spread = jnp.mean(centred * centred, axis=-1, keepdims=True)
    return centred * lax.rsqrt(spread + EPSILON) * gain


def dot(a, b):
    return jnp.dot(a, b, preferred_element_type=jnp.float32)


def pairs_of(tokens):
    return tokens.reshape(-1, Z, tokens.shape[-1])


def expand_kernel(coarse, weight, skip, surface, table, gain, attn_gain, qkv, *refs):
    position = lax.axis_index("lon")
    tokens, normed, qkv_out = refs[0:2], refs[2:4], refs[4]
    buffer, coarse_in, skip_in, surface_in, table_in, gain_in, attn_gain_in, arrived = refs[5:]
    small = [
        pltpu.make_async_copy(source, target, arrived.at[4 + at])
        for at, (source, target) in enumerate(
            (
                (coarse, coarse_in),
                (surface, surface_in),
                (table, table_in),
                (gain, gain_in),
                (attn_gain, attn_gain_in),
                (skip, skip_in),
            )
        )
    ]
    large = [
        pltpu.make_async_copy(weight.at[:, phase * D : (phase + 1) * D], buffer.at[phase], arrived.at[phase])
        for phase in range(4)
    ]
    later = pltpu.make_async_copy(qkv, qkv_out, arrived.at[10])
    for copy in (*small, *large, later):
        copy.start()
    starts = [half_start(half, position) // 2 for half in (0, 1)]
    place = lax.broadcasted_iota(jnp.int32, (72, ROWS), 0)
    lane = lax.broadcasted_iota(jnp.int32, (72, ROWS), 1)
    inside = lax.rem(place, 36)
    row = 2 * (inside // 6)
    column = 2 * (lax.rem(inside, 6) // 2 + jnp.where(place < 36, starts[0], starts[1]))
    for copy in small:
        copy.wait()

    def by_halves(part):
        return flat(jnp.concatenate([pairs_of(part(pl.ds(start, 3))) for start in starts], axis=0))

    rows = by_halves(lambda columns: coarse_in[:, columns])
    kinds = surface_in[...].astype(jnp.float32)
    added = []
    for phase in range(4):
        a, b = phase // 2, phase % 2
        picked = dot((row + a == lane).astype(jnp.float32), kinds)
        kind = jnp.sum(jnp.where(column + b == lane, picked, 0.0), axis=-1, keepdims=True)
        term = jnp.where(kind == 0, table_in[0:1], jnp.where(kind == 1, table_in[1:2], table_in[2:3]))
        added.append(by_halves(lambda columns: skip_in[:, a, columns, b]).astype(jnp.float32) + term)

    def finish(phase, expanded):
        a, b = phase // 2, phase % 2
        made = (added[phase] + normalized(expanded, gain_in[...])).astype(jnp.bfloat16)
        ready = normalized(made.astype(jnp.float32), attn_gain_in[...]).astype(jnp.bfloat16)
        for values, halves in ((made, tokens), (ready, normed)):
            values = pairs_of(values)
            halves[0][:, a, :, b] = values[:18].reshape(6, 3, Z, D)
            halves[1][:, a, :, b] = values[18:].reshape(6, 3, Z, D)

    waiting = None
    for phase in range(4):
        large[phase].wait()
        expanded = dot(rows, buffer[phase])
        if waiting is not None:
            finish(phase - 1, waiting)
        waiting = expanded
    finish(3, waiting)
    later.wait()


VMEM = pl.BlockSpec(memory_space=pltpu.VMEM)
HBM = pl.BlockSpec(memory_space=pltpu.HBM)
SMEM = pl.BlockSpec(memory_space=pltpu.SMEM)


def expand(coarse, skip, land_sea, surf_table, expand_weight, expand_gain, attn_gain, qkv_weight):
    half = jax.ShapeDtypeStruct((6, 2, 3, 2, Z, D), jnp.bfloat16)
    *halves, qkv_weight = pl.pallas_call(
        expand_kernel,
        out_shape=(half,) * 4 + (jax.ShapeDtypeStruct(qkv_weight.shape, jnp.bfloat16),),
        in_specs=[HBM] * 8,
        out_specs=(VMEM,) * 5,
        scratch_shapes=[
            pltpu.VMEM((4, CD, D), jnp.bfloat16),
            pltpu.VMEM((6, 6, Z, CD), jnp.bfloat16),
            pltpu.VMEM((6, 2, 6, 2, Z, D), jnp.bfloat16),
            pltpu.VMEM((ROWS, COLS), jnp.int32),
            pltpu.VMEM((3, D), jnp.float32),
            pltpu.VMEM((1, D), jnp.float32),
            pltpu.VMEM((1, D), jnp.float32),
            pltpu.SemaphoreType.DMA((11,)),
        ],
        compiler_params=pltpu.CompilerParams(vmem_limit_bytes=16 * MIB),
        cost_estimate=pl.CostEstimate(flops=2 * 72 * CD * 2048, bytes_accessed=5 * MIB, transcendentals=0),
        name="expand",
    )(
        *(
            pltpu.with_memory_space_constraint(operand, pltpu.HBM)
            for operand in (
                jnp.transpose(coarse, (1, 2, 0, 3)),
                expand_weight,
                jnp.transpose(skip, (1, 2, 0, 3)).reshape(6, 2, 6, 2, Z, D),
                land_sea,
                surf_table,
                expand_gain.reshape(1, D),
                attn_gain.reshape(1, D),
                qkv_weight,
            )
        )
    )
    halves = [part.reshape(ROWS, HALF, Z, D) for part in halves]
    return halves[:2], halves[2:], qkv_weight


def bf16(values):
    return values.astype(jnp.bfloat16)


def head_lanes():
    return lax.broadcasted_iota(jnp.int32, (1, 256), 1) // HEAD


def head_ones():
    return bf16((lax.broadcasted_iota(jnp.int32, (256, 256), 0) // HEAD == head_lanes()).astype(jnp.float32))


def projected(rows, weight, column):
    return bf16(dot(rows, weight[:, column : column + 256]))


def unit(rows, weight, column, ones):
    product = projected(rows, weight, column).astype(jnp.float32)
    squares = dot(bf16(product * product), ones)
    return product * lax.rsqrt(squares + 1e-06)


def scaled_queries(rows, weight, group, scale, ones):
    lane = head_lanes()
    factor = jnp.full((1, 256), scale[4 * group], jnp.float32)
    for h in range(1, 4):
        factor = jnp.where(lane == h, scale[4 * group + h], factor)
    return unit(rows, weight, 256 * group, ones) * factor


def attended(q, keys, values, live=None):
    size = q.shape[0]
    lane = head_lanes()
    stacked = bf16(jnp.concatenate([jnp.where(lane == h, q, 0.0) for h in range(4)], axis=0))
    scores = lax.dot_general(stacked, keys, (((1,), (1,)), ((), ())), preferred_element_type=jnp.float32)
    powers = jnp.exp(scores)
    if live is not None:
        powers = jnp.where(live, powers, 0.0)
    share = 1.0 / jnp.sum(powers, axis=-1, keepdims=True)
    mixed = dot(bf16(powers), values) * share
    result = jnp.where(lane == 0, mixed[:size], 0.0)
    for h in range(1, 4):
        result = jnp.where(lane == h, mixed[h * size : (h + 1) * size], result)
    return bf16(result)


def middle_kernel(
    own0, own1, mine0, mine1, beside0, beside1, weight, scale, projection, out, keys, values, queries, out_weight, every, made, blended, sent
):
    lat, lon = lax.axis_index("lat"), lax.axis_index("lon")
    middle = pl.ds(EDGE, ROWS - 2 * EDGE)
    ones = head_ones()
    fetched = pltpu.make_async_copy(projection, out_weight, sent.at[1])
    fetched.start()
    asking = []
    for half, mine, beside in ((0, mine0, beside0), (1, mine1, beside1)):
        every[144 * half : 144 * half + 144] = flat(
            jnp.concatenate([pairs_of(mine[middle]), pairs_of(beside[middle])], axis=0)
        )
        for edge in (0, 1):
            rows = pl.ds(edge_start(edge, lat), EDGE)
            at = 288 + 72 * (2 * edge + half)
            every[at : at + 72] = flat(jnp.concatenate([pairs_of(mine[rows]), pairs_of(beside[rows])], axis=0))
        asking.append(every[144 * half : 144 * half + 72])
    asking += [every[288 + 72 * at : 288 + 72 * at + 40] for at in range(4)]
    asking = bf16(jnp.concatenate([part.astype(jnp.float32) for part in asking], axis=0))
    for group in (0, 1):
        lanes = slice(256 * group, 256 * group + 256)
        query = scaled_queries(asking, weight, group, scale, ones)
        key = unit(every[...], weight, D + 256 * group, ones)
        value = projected(every[...], weight, 2 * D + 256 * group)
        for half in (0, 1):
            window = slice(144 * half, 144 * half + 144)
            blended[72 * half : 72 * half + 72, lanes] = attended(
                query[72 * half : 72 * half + 72], bf16(key[window]), value[window]
            )
        keys[:, lanes] = key[288:]
        values[:, lanes] = value[288:].astype(jnp.float32)
        queries[:, lanes] = query[144:]
    tokens = [flat(own[middle]).astype(jnp.float32) for own in (own0, own1)]
    fetched.wait()
    result = jnp.concatenate(tokens, axis=0) + dot(blended[...], out_weight[...])
    for half in (0, 1):
        made[:, pl.ds(half_start(half, lon), HALF)] = result[72 * half : 72 * half + 72].reshape(6, HALF, Z, D)
    copy = pltpu.make_async_copy(made, out.at[middle], sent.at[0])
    copy.start()
    copy.wait()


def edge_kernel(
    own0, own1, over0, seam0, over1, weight, out_weight, keys, values, queries, begun, out, made, blended, sent
):
    lat, lon = lax.axis_index("lat"), lax.axis_index("lon")
    last = lax.axis_size("lat") - 1
    ones = head_ones()
    received = []
    seam = seam_of("lat")
    at_seam = (lat == seam) | (lat == seam - 1)
    for over in (over0, over1):
        for half in (0, 1):
            part = over[2 * half : 2 * half + 2]
            if over is over0:
                part = jnp.where(at_seam, seam0[2 * half : 2 * half + 2], part)
            received.append(flat(pairs_of(part)))
    received = bf16(jnp.concatenate([part.astype(jnp.float32) for part in received], axis=0))
    paired = jnp.where((lat > 0) & (lat < last), 144, 72)
    live = lax.broadcasted_iota(jnp.int32, (1, 144), 1) < paired
    for group in (0, 1):
        lanes = slice(256 * group, 256 * group + 256)
        key = unit(received, weight, D + 256 * group, ones)
        value = projected(received, weight, 2 * D + 256 * group).astype(jnp.float32)
        for at in range(4):
            far = slice(72 * at, 72 * at + 72)
            blended[40 * at : 40 * at + 40, lanes] = attended(
                queries[40 * at : 40 * at + 40, lanes],
                bf16(jnp.concatenate([keys[far, lanes], key[far]], axis=0)),
                bf16(jnp.concatenate([values[far, lanes], value[far]], axis=0)),
                live if at >= 2 else None,
            ).astype(jnp.float32)
    result = dot(bf16(blended[...]), out_weight[...])
    copies = []
    for edge in (0, 1):
        rows = pl.ds(edge_start(edge, lat), EDGE)
        for half, own in ((0, own0), (1, own1)):
            at = 40 * (2 * edge + half)
            part = result[at : at + 40].reshape(20, Z, D)[:18].reshape(EDGE, HALF, Z, D)
            made[edge, :, pl.ds(half_start(half, lon), HALF)] = own[rows].astype(jnp.float32) + part
        copies.append(pltpu.make_async_copy(made.at[edge], out.at[rows], sent.at[edge]))
    for copy in copies:
        copy.start()
    for copy in copies:
        copy.wait()


OUT = jax.ShapeDtypeStruct((ROWS, COLS, Z, D), jnp.float32)


def middle_windows(own, mine, beside, qkv_weight, logit_scale, out_weight):
    return pl.pallas_call(
        middle_kernel,
        out_shape=(
            OUT,
            jax.ShapeDtypeStruct((288, D), jnp.float32),
            jax.ShapeDtypeStruct((288, D), jnp.float32),
            jax.ShapeDtypeStruct((160, D), jnp.float32),
            jax.ShapeDtypeStruct((D, D), jnp.bfloat16),
        ),
        in_specs=[VMEM] * 7 + [SMEM, HBM],
        out_specs=(HBM, VMEM, VMEM, VMEM, VMEM),
        scratch_shapes=[
            pltpu.VMEM((576, D), jnp.bfloat16),
            pltpu.VMEM((6, COLS, Z, D), jnp.float32),
            pltpu.VMEM((144, D), jnp.bfloat16),
            pltpu.SemaphoreType.DMA((2,)),
        ],
        compiler_params=pltpu.CompilerParams(vmem_limit_bytes=32 * MIB),
        cost_estimate=pl.CostEstimate(flops=2 << 30, bytes_accessed=2 * MIB, transcendentals=350000),
        name="middle",
    )(*own, *mine, *beside, qkv_weight, logit_scale, pltpu.with_memory_space_constraint(out_weight, pltpu.HBM))


def edge_windows(own, over, qkv_weight, begun, keys, values, queries, out_weight):
    return pl.pallas_call(
        edge_kernel,
        out_shape=OUT,
        in_specs=[VMEM] * 10 + [HBM],
        out_specs=HBM,
        scratch_shapes=[
            pltpu.VMEM((2, EDGE, COLS, Z, D), jnp.float32),
            pltpu.VMEM((160, D), jnp.float32),
            pltpu.SemaphoreType.DMA((2,)),
        ],
        input_output_aliases={10: 0},
        compiler_params=pltpu.CompilerParams(vmem_limit_bytes=32 * MIB),
        cost_estimate=pl.CostEstimate(flops=1 << 30, bytes_accessed=2 * MIB, transcendentals=350000),
        name="edges",
    )(*own, *over, qkv_weight, out_weight, keys, values, queries, begun)


def seam_of(axis):
    return lax.axis_size(axis) // 2 - 1


def swapped(value, axis, turn, ring, places=None):
    count = lax.axis_size(axis)
    pairs = []
    for source in range(count) if places is None else places:
        target = source + 1 if source % 2 == turn else source - 1
        if not ring and not 0 <= target < count:
            target = source
        pairs.append((source, target % count))
    return lax.ppermute(value, axis, pairs)


def per_device(
    coarse,
    skip_tokens,
    land_sea,
    surf_table,
    expand_weight,
    expand_gain,
    attn_gain,
    qkv_weight,
    logit_scale,
    out_weight,
):
    own, mine, qkv_weight = expand(
        coarse, skip_tokens, land_sea, surf_table, expand_weight, expand_gain, attn_gain, qkv_weight
    )
    beside = []
    for turn in (0, 1):
        beside.append(swapped(mine[turn], "lon", turn, True))
    lat = lax.axis_index("lat")

    def rows_for(turn):
        return jnp.stack(
            [
                lax.dynamic_slice_in_dim(part, edge_start(turn, lat), EDGE, 0)
                for part in (mine[0], beside[0], mine[1], beside[1])
            ]
        )

    seam = seam_of("lat")
    at_seam = [seam - 1, seam]
    rows = [rows_for(turn) for turn in (0, 1)]
    over0 = swapped(rows[0], "lat", 0, False, [at for at in range(lax.axis_size("lat")) if at not in at_seam])
    over1 = swapped(rows[1], "lat", 1, False)
    seam0 = swapped(rows[0], "lat", 0, False, at_seam)
    over = (over0, seam0, over1)
    begun, *held = middle_windows(own, mine, beside, qkv_weight, logit_scale, out_weight)
    mixed = edge_windows(own, over, qkv_weight, begun, *held)
    return jnp.transpose(mixed, (2, 0, 1, 3))


def solution(mesh):
    in_specs = (
        P(None, "lat", "lon", None),
        P(None, "lat", "lon", None),
        P("lat", "lon"),
        P(),
        P(),
        P(),
        P(),
        P(),
        P(),
        P(),
    )
    out_specs = P(None, "lat", "lon", None)
    return jax.shard_map(
        per_device, mesh=mesh, in_specs=in_specs, out_specs=out_specs, check_vma=False
    )
```

```python
import jax
import jax.numpy as jnp
from jax import lax
from jax.experimental import pallas as pl
from jax.experimental.pallas import tpu as pltpu
from jax.sharding import PartitionSpec as P


D = 512
CD = 1024
HEAD = 64
ROWS = 12
COLS = 12
HALF = 6
EDGE = 3
Z = 2
EPSILON = 1e-05
MIB = 1 << 20


def half_start(half, position):
    return HALF * ((half + position + 1) % 2)


def edge_start(edge, position):
    return (ROWS - EDGE) * ((edge + position + 1) % 2)


def flat(tokens):
    return tokens.reshape(-1, tokens.shape[-1])


def normalized(values, gain):
    average = jnp.mean(values, axis=-1, keepdims=True)
    centred = values - average
    spread = jnp.mean(centred * centred, axis=-1, keepdims=True)
    return centred * lax.rsqrt(spread + EPSILON) * gain


def dot(a, b):
    return jnp.dot(a, b, preferred_element_type=jnp.float32)


def pairs_of(tokens):
    return tokens.reshape(-1, Z, tokens.shape[-1])


def expand_kernel(coarse, weight, skip, surface, table, gain, attn_gain, qkv, *refs):
    position = lax.axis_index("lon")
    tokens, normed, qkv_out = refs[0:2], refs[2:4], refs[4]
    buffer, coarse_in, skip_in, surface_in, table_in, gain_in, attn_gain_in, arrived = refs[5:]
    small = [
        pltpu.make_async_copy(source, target, arrived.at[4 + at])
        for at, (source, target) in enumerate(
            (
                (coarse, coarse_in),
                (surface, surface_in),
                (table, table_in),
                (gain, gain_in),
                (attn_gain, attn_gain_in),
                (skip, skip_in),
            )
        )
    ]
    large = [
        pltpu.make_async_copy(weight.at[:, phase * D : (phase + 1) * D], buffer.at[phase], arrived.at[phase])
        for phase in range(4)
    ]
    later = pltpu.make_async_copy(qkv, qkv_out, arrived.at[10])
    for copy in (*small, *large, later):
        copy.start()
    starts = [half_start(half, position) // 2 for half in (0, 1)]
    place = lax.broadcasted_iota(jnp.int32, (72, ROWS), 0)
    lane = lax.broadcasted_iota(jnp.int32, (72, ROWS), 1)
    inside = lax.rem(place, 36)
    row = 2 * (inside // 6)
    column = 2 * (lax.rem(inside, 6) // 2 + jnp.where(place < 36, starts[0], starts[1]))
    for copy in small:
        copy.wait()

    def by_halves(part):
        return flat(jnp.concatenate([pairs_of(part(pl.ds(start, 3))) for start in starts], axis=0))

    rows = by_halves(lambda columns: coarse_in[:, columns])
    kinds = surface_in[...].astype(jnp.float32)
    added = []
    for phase in range(4):
        a, b = phase // 2, phase % 2
        picked = dot((row + a == lane).astype(jnp.float32), kinds)
        kind = jnp.sum(jnp.where(column + b == lane, picked, 0.0), axis=-1, keepdims=True)
        term = jnp.where(kind == 0, table_in[0:1], jnp.where(kind == 1, table_in[1:2], table_in[2:3]))
        added.append(by_halves(lambda columns: skip_in[:, a, columns, b]).astype(jnp.float32) + term)

    def finish(phase, expanded):
        a, b = phase // 2, phase % 2
        made = (added[phase] + normalized(expanded, gain_in[...])).astype(jnp.bfloat16)
        ready = normalized(made.astype(jnp.float32), attn_gain_in[...]).astype(jnp.bfloat16)
        for values, halves in ((made, tokens), (ready, normed)):
            values = pairs_of(values)
            halves[0][:, a, :, b] = values[:18].reshape(6, 3, Z, D)
            halves[1][:, a, :, b] = values[18:].reshape(6, 3, Z, D)

    waiting = None
    for phase in range(4):
        large[phase].wait()
        expanded = dot(rows, buffer[phase])
        if waiting is not None:
            finish(phase - 1, waiting)
        waiting = expanded
    finish(3, waiting)
    later.wait()


VMEM = pl.BlockSpec(memory_space=pltpu.VMEM)
HBM = pl.BlockSpec(memory_space=pltpu.HBM)
SMEM = pl.BlockSpec(memory_space=pltpu.SMEM)


def expand(coarse, skip, land_sea, surf_table, expand_weight, expand_gain, attn_gain, qkv_weight):
    half = jax.ShapeDtypeStruct((6, 2, 3, 2, Z, D), jnp.bfloat16)
    *halves, qkv_weight = pl.pallas_call(
        expand_kernel,
        out_shape=(half,) * 4 + (jax.ShapeDtypeStruct(qkv_weight.shape, jnp.bfloat16),),
        in_specs=[HBM] * 8,
        out_specs=(VMEM,) * 5,
        scratch_shapes=[
            pltpu.VMEM((4, CD, D), jnp.bfloat16),
            pltpu.VMEM((6, 6, Z, CD), jnp.bfloat16),
            pltpu.VMEM((6, 2, 6, 2, Z, D), jnp.bfloat16),
            pltpu.VMEM((ROWS, COLS), jnp.int32),
            pltpu.VMEM((3, D), jnp.float32),
            pltpu.VMEM((1, D), jnp.float32),
            pltpu.VMEM((1, D), jnp.float32),
            pltpu.SemaphoreType.DMA((11,)),
        ],
        compiler_params=pltpu.CompilerParams(vmem_limit_bytes=16 * MIB),
        cost_estimate=pl.CostEstimate(flops=2 * 72 * CD * 2048, bytes_accessed=5 * MIB, transcendentals=0),
        name="expand",
    )(
        *(
            pltpu.with_memory_space_constraint(operand, pltpu.HBM)
            for operand in (
                jnp.transpose(coarse, (1, 2, 0, 3)),
                expand_weight,
                jnp.transpose(skip, (1, 2, 0, 3)).reshape(6, 2, 6, 2, Z, D),
                land_sea,
                surf_table,
                expand_gain.reshape(1, D),
                attn_gain.reshape(1, D),
                qkv_weight,
            )
        )
    )
    halves = [part.reshape(ROWS, HALF, Z, D) for part in halves]
    return halves[:2], halves[2:], qkv_weight


def bf16(values):
    return values.astype(jnp.bfloat16)


def head_lanes():
    return lax.broadcasted_iota(jnp.int32, (1, 256), 1) // HEAD


def head_ones():
    return bf16((lax.broadcasted_iota(jnp.int32, (256, 256), 0) // HEAD == head_lanes()).astype(jnp.float32))


def projected(rows, weight, column):
    return bf16(dot(rows, weight[:, column : column + 256]))


def unit(rows, weight, column, ones):
    product = projected(rows, weight, column).astype(jnp.float32)
    squares = dot(bf16(product * product), ones)
    return product * lax.rsqrt(squares + 1e-06)


def scaled_queries(rows, weight, group, scale, ones):
    lane = head_lanes()
    factor = jnp.full((1, 256), scale[4 * group], jnp.float32)
    for h in range(1, 4):
        factor = jnp.where(lane == h, scale[4 * group + h], factor)
    return unit(rows, weight, 256 * group, ones) * factor


def attended(q, keys, values, live=None):
    size = q.shape[0]
    lane = head_lanes()
    stacked = bf16(jnp.concatenate([jnp.where(lane == h, q, 0.0) for h in range(4)], axis=0))
    scores = lax.dot_general(stacked, keys, (((1,), (1,)), ((), ())), preferred_element_type=jnp.float32)
    powers = jnp.exp(scores)
    if live is not None:
        powers = jnp.where(live, powers, 0.0)
    share = 1.0 / jnp.sum(powers, axis=-1, keepdims=True)
    mixed = dot(bf16(powers), values) * share
    result = jnp.where(lane == 0, mixed[:size], 0.0)
    for h in range(1, 4):
        result = jnp.where(lane == h, mixed[h * size : (h + 1) * size], result)
    return bf16(result)


def own_kernel(mine0, mine1, weight, scale, keys, values, queries):
    lat = lax.axis_index("lat")
    ones = head_ones()
    centre = [pairs_of(mine[pl.ds(EDGE, ROWS - 2 * EDGE)]) for mine in (mine0, mine1)]
    asking = list(centre)
    for edge in (0, 1):
        for mine in (mine0, mine1):
            asking += [pairs_of(mine[pl.ds(edge_start(edge, lat), EDGE)]), centre[0][:2]]
    asking = flat(jnp.concatenate(asking, axis=0))
    middle = asking[:144]
    for group in (0, 1):
        lanes = slice(256 * group, 256 * group + 256)
        queries[:, lanes] = scaled_queries(asking, weight, group, scale, ones)
        keys[:, lanes] = unit(middle, weight, D + 256 * group, ones)
        values[:, lanes] = projected(middle, weight, 2 * D + 256 * group).astype(jnp.float32)


def middle_kernel(
    own0, own1, mine0, mine1, beside0, beside1, weight, projection, own_keys, own_values, queries, *refs
):
    made, keys, values, out_weight, blended, sent = refs
    lat, lon = lax.axis_index("lat"), lax.axis_index("lon")
    middle = pl.ds(EDGE, ROWS - 2 * EDGE)
    ones = head_ones()
    fetched = pltpu.make_async_copy(projection, out_weight, sent)
    fetched.start()
    every = [pairs_of(beside[middle]) for beside in (beside0, beside1)]
    for edge in (0, 1):
        rows = pl.ds(edge_start(edge, lat), EDGE)
        for mine, beside in ((mine0, beside0), (mine1, beside1)):
            every += [pairs_of(mine[rows]), pairs_of(beside[rows])]
    every = flat(jnp.concatenate(every, axis=0))
    for group in (0, 1):
        lanes = slice(256 * group, 256 * group + 256)
        key = unit(every, weight, D + 256 * group, ones)
        value = projected(every, weight, 2 * D + 256 * group).astype(jnp.float32)
        for half in (0, 1):
            part = slice(72 * half, 72 * half + 72)
            blended[part, lanes] = attended(
                queries[part, lanes],
                bf16(jnp.concatenate([own_keys[part, lanes], key[part]], axis=0)),
                bf16(jnp.concatenate([own_values[part, lanes], value[part]], axis=0)),
            )
        keys[:, lanes] = key[144:]
        values[:, lanes] = value[144:]
    tokens = [flat(own[middle]).astype(jnp.float32) for own in (own0, own1)]
    fetched.wait()
    result = jnp.concatenate(tokens, axis=0) + dot(blended[...], out_weight[...])
    for half in (0, 1):
        made[:, pl.ds(half_start(half, lon), HALF)] = result[72 * half : 72 * half + 72].reshape(6, HALF, Z, D)


def edge_kernel(
    own0, own1, over0, seam0, over1, weight, out_weight, keys, values, queries, begun, out, made, blended, sent
):
    earlier = pltpu.make_async_copy(begun, out.at[pl.ds(EDGE, ROWS - 2 * EDGE)], sent.at[2])
    earlier.start()
    lat, lon = lax.axis_index("lat"), lax.axis_index("lon")
    last = lax.axis_size("lat") - 1
    ones = head_ones()
    received = []
    seam = seam_of("lat")
    at_seam = (lat == seam) | (lat == seam - 1)
    for over in (over0, over1):
        for half in (0, 1):
            part = over[2 * half : 2 * half + 2]
            if over is over0:
                part = jnp.where(at_seam, seam0[2 * half : 2 * half + 2], part)
            received.append(flat(pairs_of(part)))
    received = bf16(jnp.concatenate([part.astype(jnp.float32) for part in received], axis=0))
    paired = jnp.where((lat > 0) & (lat < last), 144, 72)
    live = lax.broadcasted_iota(jnp.int32, (1, 144), 1) < paired
    for group in (0, 1):
        lanes = slice(256 * group, 256 * group + 256)
        key = unit(received, weight, D + 256 * group, ones)
        value = projected(received, weight, 2 * D + 256 * group).astype(jnp.float32)
        for at in range(4):
            far = slice(72 * at, 72 * at + 72)
            blended[40 * at : 40 * at + 40, lanes] = attended(
                queries[144 + 40 * at : 184 + 40 * at, lanes],
                bf16(jnp.concatenate([keys[far, lanes], key[far]], axis=0)),
                bf16(jnp.concatenate([values[far, lanes], value[far]], axis=0)),
                live if at >= 2 else None,
            ).astype(jnp.float32)
    result = dot(bf16(blended[...]), out_weight[...])
    copies = [earlier]
    for edge in (0, 1):
        rows = pl.ds(edge_start(edge, lat), EDGE)
        for half, own in ((0, own0), (1, own1)):
            at = 40 * (2 * edge + half)
            part = result[at : at + 40].reshape(20, Z, D)[:18].reshape(EDGE, HALF, Z, D)
            made[edge, :, pl.ds(half_start(half, lon), HALF)] = own[rows].astype(jnp.float32) + part
        copies.append(pltpu.make_async_copy(made.at[edge], out.at[rows], sent.at[edge]))
        copies[-1].start()
    for copy in copies:
        copy.wait()


def own_parts(mine, qkv_weight, logit_scale):
    shapes = ((144, D), (144, D), (304, D))
    return pl.pallas_call(
        own_kernel,
        out_shape=tuple(jax.ShapeDtypeStruct(shape, jnp.float32) for shape in shapes),
        in_specs=[VMEM] * 3 + [SMEM],
        out_specs=(VMEM,) * 3,
        compiler_params=pltpu.CompilerParams(vmem_limit_bytes=32 * MIB),
        cost_estimate=pl.CostEstimate(flops=1 << 30, bytes_accessed=2 * MIB, transcendentals=0),
        name="own",
    )(*mine, qkv_weight, logit_scale)


def middle_windows(own, mine, beside, qkv_weight, out_weight, keys, values, queries):
    return pl.pallas_call(
        middle_kernel,
        out_shape=(
            jax.ShapeDtypeStruct((6, COLS, Z, D), jnp.float32),
            jax.ShapeDtypeStruct((288, D), jnp.float32),
            jax.ShapeDtypeStruct((288, D), jnp.float32),
            jax.ShapeDtypeStruct((D, D), jnp.bfloat16),
        ),
        in_specs=[VMEM] * 7 + [HBM] + [VMEM] * 3,
        out_specs=(VMEM,) * 4,
        scratch_shapes=[pltpu.VMEM((144, D), jnp.bfloat16), pltpu.SemaphoreType.DMA(())],
        compiler_params=pltpu.CompilerParams(vmem_limit_bytes=32 * MIB),
        cost_estimate=pl.CostEstimate(flops=2 << 30, bytes_accessed=2 * MIB, transcendentals=350000),
        name="middle",
    )(
        *own,
        *mine,
        *beside,
        qkv_weight,
        pltpu.with_memory_space_constraint(out_weight, pltpu.HBM),
        keys,
        values,
        queries,
    )


def edge_windows(own, over, qkv_weight, begun, keys, values, queries, out_weight):
    return pl.pallas_call(
        edge_kernel,
        out_shape=jax.ShapeDtypeStruct((ROWS, COLS, Z, D), jnp.float32),
        in_specs=[VMEM] * 11,
        out_specs=HBM,
        scratch_shapes=[
            pltpu.VMEM((2, EDGE, COLS, Z, D), jnp.float32),
            pltpu.VMEM((160, D), jnp.float32),
            pltpu.SemaphoreType.DMA((3,)),
        ],
        compiler_params=pltpu.CompilerParams(vmem_limit_bytes=32 * MIB),
        cost_estimate=pl.CostEstimate(flops=1 << 30, bytes_accessed=2 * MIB, transcendentals=350000),
        name="edges",
    )(*own, *over, qkv_weight, out_weight, keys, values, queries, begun)


def seam_of(axis):
    return lax.axis_size(axis) // 2 - 1


def swapped(value, axis, turn, ring, places=None):
    count = lax.axis_size(axis)
    pairs = []
    for source in range(count) if places is None else places:
        target = source + 1 if source % 2 == turn else source - 1
        if not ring and not 0 <= target < count:
            target = source
        pairs.append((source, target % count))
    return lax.ppermute(value, axis, pairs)


def per_device(
    coarse,
    skip_tokens,
    land_sea,
    surf_table,
    expand_weight,
    expand_gain,
    attn_gain,
    qkv_weight,
    logit_scale,
    out_weight,
):
    own, mine, qkv_weight = expand(
        coarse, skip_tokens, land_sea, surf_table, expand_weight, expand_gain, attn_gain, qkv_weight
    )
    own_keys, own_values, queries = own_parts(mine, qkv_weight, logit_scale)
    beside = []
    for turn in (0, 1):
        beside.append(swapped(mine[turn], "lon", turn, True))
    lat = lax.axis_index("lat")

    def rows_for(turn):
        return jnp.stack(
            [
                lax.dynamic_slice_in_dim(part, edge_start(turn, lat), EDGE, 0)
                for part in (mine[0], beside[0], mine[1], beside[1])
            ]
        )

    seam = seam_of("lat")
    at_seam = [seam - 1, seam]
    rows = [rows_for(turn) for turn in (0, 1)]
    over0 = swapped(rows[0], "lat", 0, False, [at for at in range(lax.axis_size("lat")) if at not in at_seam])
    over1 = swapped(rows[1], "lat", 1, False)
    seam0 = swapped(rows[0], "lat", 0, False, at_seam)
    over = (over0, seam0, over1)
    begun, keys, values, out_weight = middle_windows(
        own, mine, beside, qkv_weight, out_weight, own_keys, own_values, queries
    )
    mixed = edge_windows(own, over, qkv_weight, begun, keys, values, queries, out_weight)
    return jnp.transpose(mixed, (2, 0, 1, 3))


def solution(mesh):
    in_specs = (
        P(None, "lat", "lon", None),
        P(None, "lat", "lon", None),
        P("lat", "lon"),
        P(),
        P(),
        P(),
        P(),
        P(),
        P(),
        P(),
    )
    out_specs = P(None, "lat", "lon", None)
    return jax.shard_map(
        per_device, mesh=mesh, in_specs=in_specs, out_specs=out_specs, check_vma=False
    )
```

```python
import jax
import jax.numpy as jnp
from jax import lax
from jax.experimental import pallas as pl
from jax.experimental.pallas import tpu as pltpu
from jax.sharding import PartitionSpec as P


D = 512
CD = 1024
HEAD = 64
ROWS = 12
COLS = 12
HALF = 6
EDGE = 3
Z = 2
EPSILON = 1e-05
MIB = 1 << 20


def half_start(half, position):
    return HALF * ((half + position + 1) % 2)


def edge_start(edge, position):
    return (ROWS - EDGE) * ((edge + position + 1) % 2)


def flat(tokens):
    return tokens.reshape(-1, tokens.shape[-1])


def normalized(values, gain):
    average = jnp.mean(values, axis=-1, keepdims=True)
    centred = values - average
    spread = jnp.mean(centred * centred, axis=-1, keepdims=True)
    return centred * lax.rsqrt(spread + EPSILON) * gain


def dot(a, b):
    return jnp.dot(a, b, preferred_element_type=jnp.float32)


def pairs_of(tokens):
    return tokens.reshape(-1, Z, tokens.shape[-1])


def expand_kernel(coarse, weight, skip, surface, table, gain, attn_gain, qkv, *refs):
    position = lax.axis_index("lon")
    tokens, normed, qkv_out = refs[0:2], refs[2:4], refs[4]
    buffer, coarse_in, skip_in, surface_in, table_in, gain_in, attn_gain_in, arrived = refs[5:]
    small = [
        pltpu.make_async_copy(source, target, arrived.at[4 + at])
        for at, (source, target) in enumerate(
            (
                (coarse, coarse_in),
                (surface, surface_in),
                (table, table_in),
                (gain, gain_in),
                (attn_gain, attn_gain_in),
                (skip, skip_in),
            )
        )
    ]
    large = [
        pltpu.make_async_copy(weight.at[:, phase * D : (phase + 1) * D], buffer.at[phase], arrived.at[phase])
        for phase in range(4)
    ]
    later = pltpu.make_async_copy(qkv, qkv_out, arrived.at[10])
    for copy in (*small, *large, later):
        copy.start()
    starts = [half_start(half, position) // 2 for half in (0, 1)]
    place = lax.broadcasted_iota(jnp.int32, (72, ROWS), 0)
    lane = lax.broadcasted_iota(jnp.int32, (72, ROWS), 1)
    inside = lax.rem(place, 36)
    row = 2 * (inside // 6)
    column = 2 * (lax.rem(inside, 6) // 2 + jnp.where(place < 36, starts[0], starts[1]))
    for copy in small:
        copy.wait()

    def by_halves(part):
        return flat(jnp.concatenate([pairs_of(part(pl.ds(start, 3))) for start in starts], axis=0))

    rows = by_halves(lambda columns: coarse_in[:, columns])
    kinds = surface_in[...].astype(jnp.float32)
    added = []
    for phase in range(4):
        a, b = phase // 2, phase % 2
        picked = dot((row + a == lane).astype(jnp.float32), kinds)
        kind = jnp.sum(jnp.where(column + b == lane, picked, 0.0), axis=-1, keepdims=True)
        term = jnp.where(kind == 0, table_in[0:1], jnp.where(kind == 1, table_in[1:2], table_in[2:3]))
        added.append(by_halves(lambda columns: skip_in[:, a, columns, b]).astype(jnp.float32) + term)

    def finish(phase, expanded):
        a, b = phase // 2, phase % 2
        made = (added[phase] + normalized(expanded, gain_in[...])).astype(jnp.bfloat16)
        ready = normalized(made.astype(jnp.float32), attn_gain_in[...]).astype(jnp.bfloat16)
        for values, halves in ((made, tokens), (ready, normed)):
            values = pairs_of(values)
            halves[0][:, a, :, b] = values[:18].reshape(6, 3, Z, D)
            halves[1][:, a, :, b] = values[18:].reshape(6, 3, Z, D)

    waiting = None
    for phase in range(4):
        large[phase].wait()
        expanded = dot(rows, buffer[phase])
        if waiting is not None:
            finish(phase - 1, waiting)
        waiting = expanded
    finish(3, waiting)
    later.wait()


VMEM = pl.BlockSpec(memory_space=pltpu.VMEM)
HBM = pl.BlockSpec(memory_space=pltpu.HBM)
SMEM = pl.BlockSpec(memory_space=pltpu.SMEM)


def expand(coarse, skip, land_sea, surf_table, expand_weight, expand_gain, attn_gain, qkv_weight):
    half = jax.ShapeDtypeStruct((6, 2, 3, 2, Z, D), jnp.bfloat16)
    *halves, qkv_weight = pl.pallas_call(
        expand_kernel,
        out_shape=(half,) * 4 + (jax.ShapeDtypeStruct(qkv_weight.shape, jnp.bfloat16),),
        in_specs=[HBM] * 8,
        out_specs=(VMEM,) * 5,
        scratch_shapes=[
            pltpu.VMEM((4, CD, D), jnp.bfloat16),
            pltpu.VMEM((6, 6, Z, CD), jnp.bfloat16),
            pltpu.VMEM((6, 2, 6, 2, Z, D), jnp.bfloat16),
            pltpu.VMEM((ROWS, COLS), jnp.int32),
            pltpu.VMEM((3, D), jnp.float32),
            pltpu.VMEM((1, D), jnp.float32),
            pltpu.VMEM((1, D), jnp.float32),
            pltpu.SemaphoreType.DMA((11,)),
        ],
        compiler_params=pltpu.CompilerParams(vmem_limit_bytes=16 * MIB),
        cost_estimate=pl.CostEstimate(flops=2 * 72 * CD * 2048, bytes_accessed=5 * MIB, transcendentals=0),
        name="expand",
    )(
        *(
            pltpu.with_memory_space_constraint(operand, pltpu.HBM)
            for operand in (
                jnp.transpose(coarse, (1, 2, 0, 3)),
                expand_weight,
                jnp.transpose(skip, (1, 2, 0, 3)).reshape(6, 2, 6, 2, Z, D),
                land_sea,
                surf_table,
                expand_gain.reshape(1, D),
                attn_gain.reshape(1, D),
                qkv_weight,
            )
        )
    )
    halves = [part.reshape(ROWS, HALF, Z, D) for part in halves]
    return halves[:2], halves[2:], qkv_weight


def bf16(values):
    return values.astype(jnp.bfloat16)


def head_lanes():
    return lax.broadcasted_iota(jnp.int32, (1, 256), 1) // HEAD


def head_ones():
    return bf16((lax.broadcasted_iota(jnp.int32, (256, 256), 0) // HEAD == head_lanes()).astype(jnp.float32))


def projected(rows, weight, column):
    return bf16(dot(rows, weight[:, column : column + 256]))


def unit(rows, weight, column, ones):
    product = projected(rows, weight, column).astype(jnp.float32)
    squares = dot(bf16(product * product), ones)
    return product * lax.rsqrt(squares + 1e-06)


def scaled_queries(rows, weight, group, scale, ones):
    lane = head_lanes()
    factor = jnp.full((1, 256), scale[4 * group], jnp.float32)
    for h in range(1, 4):
        factor = jnp.where(lane == h, scale[4 * group + h], factor)
    return unit(rows, weight, 256 * group, ones) * factor


def attended(q, keys, values, live=None):
    size = q.shape[0]
    lane = head_lanes()
    stacked = bf16(jnp.concatenate([jnp.where(lane == h, q, 0.0) for h in range(4)], axis=0))
    scores = lax.dot_general(stacked, keys, (((1,), (1,)), ((), ())), preferred_element_type=jnp.float32)
    powers = jnp.exp(scores)
    if live is not None:
        powers = jnp.where(live, powers, 0.0)
    share = 1.0 / jnp.sum(powers, axis=-1, keepdims=True)
    mixed = dot(bf16(powers), values) * share
    result = jnp.where(lane == 0, mixed[:size], 0.0)
    for h in range(1, 4):
        result = jnp.where(lane == h, mixed[h * size : (h + 1) * size], result)
    return bf16(result)


def middle_kernel(own0, own1, mine0, mine1, beside0, beside1, weight, scale, projection, *refs):
    made, keys, values, queries, out_weight, blended, sent = refs
    lat, lon = lax.axis_index("lat"), lax.axis_index("lon")
    middle = pl.ds(EDGE, ROWS - 2 * EDGE)
    ones = head_ones()
    fetched = pltpu.make_async_copy(projection, out_weight, sent)
    fetched.start()
    every, asking = [], []
    for mine, beside in ((mine0, beside0), (mine1, beside1)):
        asking.append(pairs_of(mine[middle]))
        every += [asking[-1], pairs_of(beside[middle])]
    for edge in (0, 1):
        rows = pl.ds(edge_start(edge, lat), EDGE)
        for mine, beside in ((mine0, beside0), (mine1, beside1)):
            asking += [pairs_of(mine[rows]), asking[0][:2]]
            every += [pairs_of(mine[rows]), pairs_of(beside[rows])]
    every = flat(jnp.concatenate(every, axis=0))
    asking = flat(jnp.concatenate(asking, axis=0))
    for group in (0, 1):
        lanes = slice(256 * group, 256 * group + 256)
        query = scaled_queries(asking, weight, group, scale, ones)
        key = unit(every, weight, D + 256 * group, ones)
        value = projected(every, weight, 2 * D + 256 * group)
        for half in (0, 1):
            window = slice(144 * half, 144 * half + 144)
            blended[72 * half : 72 * half + 72, lanes] = attended(
                query[72 * half : 72 * half + 72], bf16(key[window]), value[window]
            )
        keys[:, lanes] = key[288:]
        values[:, lanes] = value[288:].astype(jnp.float32)
        queries[:, lanes] = query[144:]
    tokens = [flat(own[middle]).astype(jnp.float32) for own in (own0, own1)]
    fetched.wait()
    result = jnp.concatenate(tokens, axis=0) + dot(blended[...], out_weight[...])
    for half in (0, 1):
        made[:, pl.ds(half_start(half, lon), HALF)] = result[72 * half : 72 * half + 72].reshape(6, HALF, Z, D)


def edge_kernel(
    own0, own1, over0, seam0, over1, weight, out_weight, keys, values, queries, begun, out, made, blended, sent
):
    earlier = pltpu.make_async_copy(begun, out.at[pl.ds(EDGE, ROWS - 2 * EDGE)], sent.at[2])
    earlier.start()
    lat, lon = lax.axis_index("lat"), lax.axis_index("lon")
    last = lax.axis_size("lat") - 1
    ones = head_ones()
    received = []
    seam = seam_of("lat")
    at_seam = (lat == seam) | (lat == seam - 1)
    for over in (over0, over1):
        for half in (0, 1):
            part = over[2 * half : 2 * half + 2]
            if over is over0:
                part = jnp.where(at_seam, seam0[2 * half : 2 * half + 2], part)
            received.append(flat(pairs_of(part)))
    received = bf16(jnp.concatenate([part.astype(jnp.float32) for part in received], axis=0))
    paired = jnp.where((lat > 0) & (lat < last), 144, 72)
    live = lax.broadcasted_iota(jnp.int32, (1, 144), 1) < paired
    for group in (0, 1):
        lanes = slice(256 * group, 256 * group + 256)
        key = unit(received, weight, D + 256 * group, ones)
        value = projected(received, weight, 2 * D + 256 * group).astype(jnp.float32)
        for at in range(4):
            far = slice(72 * at, 72 * at + 72)
            blended[40 * at : 40 * at + 40, lanes] = attended(
                queries[40 * at : 40 * at + 40, lanes],
                bf16(jnp.concatenate([keys[far, lanes], key[far]], axis=0)),
                bf16(jnp.concatenate([values[far, lanes], value[far]], axis=0)),
                live if at >= 2 else None,
            ).astype(jnp.float32)
    result = dot(bf16(blended[...]), out_weight[...])
    copies = [earlier]
    for edge in (0, 1):
        rows = pl.ds(edge_start(edge, lat), EDGE)
        for half, own in ((0, own0), (1, own1)):
            at = 40 * (2 * edge + half)
            part = result[at : at + 40].reshape(20, Z, D)[:18].reshape(EDGE, HALF, Z, D)
            made[edge, :, pl.ds(half_start(half, lon), HALF)] = own[rows].astype(jnp.float32) + part
        copies.append(pltpu.make_async_copy(made.at[edge], out.at[rows], sent.at[edge]))
        copies[-1].start()
    for copy in copies:
        copy.wait()


def pack_kernel(mine0, mine1, beside0, beside1, rows0, rows1):
    lat = lax.axis_index("lat")
    for turn, rows in ((0, rows0), (1, rows1)):
        edge = pl.ds(edge_start(turn, lat), EDGE)
        for at, part in enumerate((mine0, beside0, mine1, beside1)):
            rows[at] = part[edge]


def edge_rows(mine, beside):
    return pl.pallas_call(
        pack_kernel,
        out_shape=(jax.ShapeDtypeStruct((4, EDGE, HALF, Z, D), jnp.bfloat16),) * 2,
        in_specs=[VMEM] * 4,
        out_specs=(VMEM,) * 2,
        compiler_params=pltpu.CompilerParams(vmem_limit_bytes=8 * MIB),
        cost_estimate=pl.CostEstimate(flops=1000, bytes_accessed=MIB // 4, transcendentals=0),
        name="pack",
    )(*mine, *beside)


def middle_windows(own, mine, beside, qkv_weight, logit_scale, out_weight):
    return pl.pallas_call(
        middle_kernel,
        out_shape=(
            jax.ShapeDtypeStruct((6, COLS, Z, D), jnp.float32),
            jax.ShapeDtypeStruct((288, D), jnp.float32),
            jax.ShapeDtypeStruct((288, D), jnp.float32),
            jax.ShapeDtypeStruct((160, D), jnp.float32),
            jax.ShapeDtypeStruct((D, D), jnp.bfloat16),
        ),
        in_specs=[VMEM] * 7 + [SMEM, HBM],
        out_specs=(VMEM,) * 5,
        scratch_shapes=[pltpu.VMEM((144, D), jnp.bfloat16), pltpu.SemaphoreType.DMA(())],
        compiler_params=pltpu.CompilerParams(vmem_limit_bytes=32 * MIB),
        cost_estimate=pl.CostEstimate(flops=2 << 30, bytes_accessed=2 * MIB, transcendentals=350000),
        name="middle",
    )(
        *own,
        *mine,
        *beside,
        qkv_weight,
        logit_scale,
        pltpu.with_memory_space_constraint(out_weight, pltpu.HBM),
    )


def edge_windows(own, over, qkv_weight, begun, keys, values, queries, out_weight):
    return pl.pallas_call(
        edge_kernel,
        out_shape=jax.ShapeDtypeStruct((ROWS, COLS, Z, D), jnp.float32),
        in_specs=[VMEM] * 11,
        out_specs=HBM,
        scratch_shapes=[
            pltpu.VMEM((2, EDGE, COLS, Z, D), jnp.float32),
            pltpu.VMEM((160, D), jnp.float32),
            pltpu.SemaphoreType.DMA((3,)),
        ],
        compiler_params=pltpu.CompilerParams(vmem_limit_bytes=32 * MIB),
        cost_estimate=pl.CostEstimate(flops=1 << 30, bytes_accessed=2 * MIB, transcendentals=350000),
        name="edges",
    )(*own, *over, qkv_weight, out_weight, keys, values, queries, begun)


def seam_of(axis):
    return lax.axis_size(axis) // 2 - 1


def swapped(value, axis, turn, ring, places=None):
    count = lax.axis_size(axis)
    pairs = []
    for source in range(count) if places is None else places:
        target = source + 1 if source % 2 == turn else source - 1
        if not ring and not 0 <= target < count:
            target = source
        pairs.append((source, target % count))
    return lax.ppermute(value, axis, pairs)


def per_device(
    coarse,
    skip_tokens,
    land_sea,
    surf_table,
    expand_weight,
    expand_gain,
    attn_gain,
    qkv_weight,
    logit_scale,
    out_weight,
):
    own, mine, qkv_weight = expand(
        coarse, skip_tokens, land_sea, surf_table, expand_weight, expand_gain, attn_gain, qkv_weight
    )
    beside = []
    for turn in (0, 1):
        beside.append(swapped(mine[turn], "lon", turn, True))
    seam = seam_of("lat")
    at_seam = [seam - 1, seam]
    rows = edge_rows(mine, beside)
    over0 = swapped(rows[0], "lat", 0, False, [at for at in range(lax.axis_size("lat")) if at not in at_seam])
    over1 = swapped(rows[1], "lat", 1, False)
    seam0 = swapped(rows[0], "lat", 0, False, at_seam)
    over = (over0, seam0, over1)
    begun, keys, values, queries, out_weight = middle_windows(own, mine, beside, qkv_weight, logit_scale, out_weight)
    mixed = edge_windows(own, over, qkv_weight, begun, keys, values, queries, out_weight)
    return jnp.transpose(mixed, (2, 0, 1, 3))


def solution(mesh):
    in_specs = (
        P(None, "lat", "lon", None),
        P(None, "lat", "lon", None),
        P("lat", "lon"),
        P(),
        P(),
        P(),
        P(),
        P(),
        P(),
        P(),
    )
    out_specs = P(None, "lat", "lon", None)
    return jax.shard_map(
        per_device, mesh=mesh, in_specs=in_specs, out_specs=out_specs, check_vma=False
    )
```

```python
import jax
import jax.numpy as jnp
from jax import lax
from jax.experimental import pallas as pl
from jax.experimental.pallas import tpu as pltpu
from jax.sharding import PartitionSpec as P


D = 512
CD = 1024
HEAD = 64
ROWS = 12
COLS = 12
HALF = 6
EDGE = 3
Z = 2
EPSILON = 1e-05
MIB = 1 << 20


def half_start(half, position):
    return HALF * ((half + position + 1) % 2)


def edge_start(edge, position):
    return (ROWS - EDGE) * ((edge + position + 1) % 2)


def flat(tokens):
    return tokens.reshape(-1, tokens.shape[-1])


def normalized(values, gain):
    average = jnp.mean(values, axis=-1, keepdims=True)
    centred = values - average
    spread = jnp.mean(centred * centred, axis=-1, keepdims=True)
    return centred * lax.rsqrt(spread + EPSILON) * gain


def dot(a, b):
    return jnp.dot(a, b, preferred_element_type=jnp.float32)


def pairs_of(tokens):
    return tokens.reshape(-1, Z, tokens.shape[-1])


def expand_kernel(coarse, weight, skip, surface, table, gain, attn_gain, qkv, *refs):
    position = lax.axis_index("lon")
    tokens, normed, qkv_out = refs[0:2], refs[2:4], refs[4]
    buffer, coarse_in, skip_in, surface_in, table_in, gain_in, attn_gain_in, arrived = refs[5:]
    small = [
        pltpu.make_async_copy(source, target, arrived.at[4 + at])
        for at, (source, target) in enumerate(
            (
                (coarse, coarse_in),
                (surface, surface_in),
                (table, table_in),
                (gain, gain_in),
                (attn_gain, attn_gain_in),
                (skip, skip_in),
            )
        )
    ]
    large = [
        pltpu.make_async_copy(weight.at[:, phase * D : (phase + 1) * D], buffer.at[phase], arrived.at[phase])
        for phase in range(4)
    ]
    later = pltpu.make_async_copy(qkv, qkv_out, arrived.at[10])
    for copy in (*small, *large, later):
        copy.start()
    starts = [half_start(half, position) // 2 for half in (0, 1)]
    place = lax.broadcasted_iota(jnp.int32, (72, ROWS), 0)
    lane = lax.broadcasted_iota(jnp.int32, (72, ROWS), 1)
    inside = lax.rem(place, 36)
    row = 2 * (inside // 6)
    column = 2 * (lax.rem(inside, 6) // 2 + jnp.where(place < 36, starts[0], starts[1]))
    for copy in small:
        copy.wait()

    def by_halves(part):
        return flat(jnp.concatenate([pairs_of(part(pl.ds(start, 3))) for start in starts], axis=0))

    rows = by_halves(lambda columns: coarse_in[:, columns])
    kinds = surface_in[...].astype(jnp.float32)
    added = []
    for phase in range(4):
        a, b = phase // 2, phase % 2
        picked = dot((row + a == lane).astype(jnp.float32), kinds)
        kind = jnp.sum(jnp.where(column + b == lane, picked, 0.0), axis=-1, keepdims=True)
        term = jnp.where(kind == 0, table_in[0:1], jnp.where(kind == 1, table_in[1:2], table_in[2:3]))
        added.append(by_halves(lambda columns: skip_in[:, a, columns, b]).astype(jnp.float32) + term)

    def finish(phase, expanded):
        a, b = phase // 2, phase % 2
        made = (added[phase] + normalized(expanded, gain_in[...])).astype(jnp.bfloat16)
        ready = normalized(made.astype(jnp.float32), attn_gain_in[...]).astype(jnp.bfloat16)
        for values, halves in ((made, tokens), (ready, normed)):
            values = pairs_of(values)
            halves[0][:, a, :, b] = values[:18].reshape(6, 3, Z, D)
            halves[1][:, a, :, b] = values[18:].reshape(6, 3, Z, D)

    waiting = None
    for phase in range(4):
        large[phase].wait()
        expanded = dot(rows, buffer[phase])
        if waiting is not None:
            finish(phase - 1, waiting)
        waiting = expanded
    finish(3, waiting)
    later.wait()


VMEM = pl.BlockSpec(memory_space=pltpu.VMEM)
HBM = pl.BlockSpec(memory_space=pltpu.HBM)
SMEM = pl.BlockSpec(memory_space=pltpu.SMEM)


def expand(coarse, skip, land_sea, surf_table, expand_weight, expand_gain, attn_gain, qkv_weight):
    half = jax.ShapeDtypeStruct((6, 2, 3, 2, Z, D), jnp.bfloat16)
    *halves, qkv_weight = pl.pallas_call(
        expand_kernel,
        out_shape=(half,) * 4 + (jax.ShapeDtypeStruct(qkv_weight.shape, jnp.bfloat16),),
        in_specs=[HBM] * 8,
        out_specs=(VMEM,) * 5,
        scratch_shapes=[
            pltpu.VMEM((4, CD, D), jnp.bfloat16),
            pltpu.VMEM((6, 6, Z, CD), jnp.bfloat16),
            pltpu.VMEM((6, 2, 6, 2, Z, D), jnp.bfloat16),
            pltpu.VMEM((ROWS, COLS), jnp.int32),
            pltpu.VMEM((3, D), jnp.float32),
            pltpu.VMEM((1, D), jnp.float32),
            pltpu.VMEM((1, D), jnp.float32),
            pltpu.SemaphoreType.DMA((11,)),
        ],
        compiler_params=pltpu.CompilerParams(vmem_limit_bytes=16 * MIB),
        cost_estimate=pl.CostEstimate(flops=2 * 72 * CD * 2048, bytes_accessed=5 * MIB, transcendentals=0),
        name="expand",
    )(
        *(
            pltpu.with_memory_space_constraint(operand, pltpu.HBM)
            for operand in (
                jnp.transpose(coarse, (1, 2, 0, 3)),
                expand_weight,
                jnp.transpose(skip, (1, 2, 0, 3)).reshape(6, 2, 6, 2, Z, D),
                land_sea,
                surf_table,
                expand_gain.reshape(1, D),
                attn_gain.reshape(1, D),
                qkv_weight,
            )
        )
    )
    halves = [part.reshape(ROWS, HALF, Z, D) for part in halves]
    return halves[:2], halves[2:], qkv_weight


def bf16(values):
    return values.astype(jnp.bfloat16)


def head_lanes():
    return lax.broadcasted_iota(jnp.int32, (1, 256), 1) // HEAD


def head_ones():
    return bf16((lax.broadcasted_iota(jnp.int32, (256, 256), 0) // HEAD == head_lanes()).astype(jnp.float32))


def projected(rows, weight, column):
    return bf16(dot(rows, weight[:, column : column + 256]))


def unit(rows, weight, column, ones):
    product = projected(rows, weight, column).astype(jnp.float32)
    squares = dot(bf16(product * product), ones)
    return product * lax.rsqrt(squares + 1e-06)


def scaled_queries(rows, weight, group, scale, ones):
    lane = head_lanes()
    factor = jnp.full((1, 256), scale[4 * group], jnp.float32)
    for h in range(1, 4):
        factor = jnp.where(lane == h, scale[4 * group + h], factor)
    return unit(rows, weight, 256 * group, ones) * factor


def attended(q, keys, values, live=None):
    size = q.shape[0]
    lane = head_lanes()
    stacked = bf16(jnp.concatenate([jnp.where(lane == h, q, 0.0) for h in range(4)], axis=0))
    scores = lax.dot_general(stacked, keys, (((1,), (1,)), ((), ())), preferred_element_type=jnp.float32)
    powers = jnp.exp(scores)
    if live is not None:
        powers = jnp.where(live, powers, 0.0)
    share = 1.0 / jnp.sum(powers, axis=-1, keepdims=True)
    mixed = dot(bf16(powers), values) * share
    result = jnp.where(lane == 0, mixed[:size], 0.0)
    for h in range(1, 4):
        result = jnp.where(lane == h, mixed[h * size : (h + 1) * size], result)
    return bf16(result)


def query_kernel(mine0, mine1, weight, scale, queries):
    lat = lax.axis_index("lat")
    ones = head_ones()
    asking = [pairs_of(mine[pl.ds(EDGE, ROWS - 2 * EDGE)]) for mine in (mine0, mine1)]
    for edge in (0, 1):
        for mine in (mine0, mine1):
            asking += [pairs_of(mine[pl.ds(edge_start(edge, lat), EDGE)]), asking[0][:2]]
    asking = flat(jnp.concatenate(asking, axis=0))
    for group in (0, 1):
        queries[:, 256 * group : 256 * group + 256] = scaled_queries(asking, weight, group, scale, ones)


def middle_kernel(own0, own1, mine0, mine1, beside0, beside1, weight, projection, queries, *refs):
    made, keys, values, out_weight, blended, sent = refs
    lat, lon = lax.axis_index("lat"), lax.axis_index("lon")
    middle = pl.ds(EDGE, ROWS - 2 * EDGE)
    ones = head_ones()
    fetched = pltpu.make_async_copy(projection, out_weight, sent)
    fetched.start()
    every = []
    for mine, beside in ((mine0, beside0), (mine1, beside1)):
        every += [pairs_of(mine[middle]), pairs_of(beside[middle])]
    for edge in (0, 1):
        rows = pl.ds(edge_start(edge, lat), EDGE)
        for mine, beside in ((mine0, beside0), (mine1, beside1)):
            every += [pairs_of(mine[rows]), pairs_of(beside[rows])]
    every = flat(jnp.concatenate(every, axis=0))
    for group in (0, 1):
        lanes = slice(256 * group, 256 * group + 256)
        key = unit(every, weight, D + 256 * group, ones)
        value = projected(every, weight, 2 * D + 256 * group)
        for half in (0, 1):
            window = slice(144 * half, 144 * half + 144)
            blended[72 * half : 72 * half + 72, lanes] = attended(
                queries[72 * half : 72 * half + 72, lanes], bf16(key[window]), value[window]
            )
        keys[:, lanes] = key[288:]
        values[:, lanes] = value[288:].astype(jnp.float32)
    tokens = [flat(own[middle]).astype(jnp.float32) for own in (own0, own1)]
    fetched.wait()
    result = jnp.concatenate(tokens, axis=0) + dot(blended[...], out_weight[...])
    for half in (0, 1):
        made[:, pl.ds(half_start(half, lon), HALF)] = result[72 * half : 72 * half + 72].reshape(6, HALF, Z, D)


def edge_kernel(
    own0, own1, over0, seam0, over1, weight, out_weight, keys, values, queries, begun, out, made, blended, sent
):
    earlier = pltpu.make_async_copy(begun, out.at[pl.ds(EDGE, ROWS - 2 * EDGE)], sent.at[2])
    earlier.start()
    lat, lon = lax.axis_index("lat"), lax.axis_index("lon")
    last = lax.axis_size("lat") - 1
    ones = head_ones()
    received = []
    seam = seam_of("lat")
    at_seam = (lat == seam) | (lat == seam - 1)
    for over in (over0, over1):
        for half in (0, 1):
            part = over[2 * half : 2 * half + 2]
            if over is over0:
                part = jnp.where(at_seam, seam0[2 * half : 2 * half + 2], part)
            received.append(flat(pairs_of(part)))
    received = bf16(jnp.concatenate([part.astype(jnp.float32) for part in received], axis=0))
    paired = jnp.where((lat > 0) & (lat < last), 144, 72)
    live = lax.broadcasted_iota(jnp.int32, (1, 144), 1) < paired
    for group in (0, 1):
        lanes = slice(256 * group, 256 * group + 256)
        key = unit(received, weight, D + 256 * group, ones)
        value = projected(received, weight, 2 * D + 256 * group).astype(jnp.float32)
        for at in range(4):
            far = slice(72 * at, 72 * at + 72)
            blended[40 * at : 40 * at + 40, lanes] = attended(
                queries[144 + 40 * at : 184 + 40 * at, lanes],
                bf16(jnp.concatenate([keys[far, lanes], key[far]], axis=0)),
                bf16(jnp.concatenate([values[far, lanes], value[far]], axis=0)),
                live if at >= 2 else None,
            ).astype(jnp.float32)
    result = dot(bf16(blended[...]), out_weight[...])
    copies = [earlier]
    for edge in (0, 1):
        rows = pl.ds(edge_start(edge, lat), EDGE)
        for half, own in ((0, own0), (1, own1)):
            at = 40 * (2 * edge + half)
            part = result[at : at + 40].reshape(20, Z, D)[:18].reshape(EDGE, HALF, Z, D)
            made[edge, :, pl.ds(half_start(half, lon), HALF)] = own[rows].astype(jnp.float32) + part
        copies.append(pltpu.make_async_copy(made.at[edge], out.at[rows], sent.at[edge]))
        copies[-1].start()
    for copy in copies:
        copy.wait()


def pack_kernel(mine0, mine1, beside0, beside1, rows0, rows1):
    lat = lax.axis_index("lat")
    for turn, rows in ((0, rows0), (1, rows1)):
        edge = pl.ds(edge_start(turn, lat), EDGE)
        for at, part in enumerate((mine0, beside0, mine1, beside1)):
            rows[at] = part[edge]


def edge_rows(mine, beside):
    return pl.pallas_call(
        pack_kernel,
        out_shape=(jax.ShapeDtypeStruct((4, EDGE, HALF, Z, D), jnp.bfloat16),) * 2,
        in_specs=[VMEM] * 4,
        out_specs=(VMEM,) * 2,
        compiler_params=pltpu.CompilerParams(vmem_limit_bytes=8 * MIB),
        cost_estimate=pl.CostEstimate(flops=1000, bytes_accessed=MIB // 4, transcendentals=0),
        name="pack",
    )(*mine, *beside)


def own_queries(mine, qkv_weight, logit_scale):
    return pl.pallas_call(
        query_kernel,
        out_shape=jax.ShapeDtypeStruct((304, D), jnp.float32),
        in_specs=[VMEM] * 3 + [SMEM],
        out_specs=VMEM,
        compiler_params=pltpu.CompilerParams(vmem_limit_bytes=16 * MIB),
        cost_estimate=pl.CostEstimate(flops=1 << 28, bytes_accessed=MIB, transcendentals=0),
        name="queries",
    )(*mine, qkv_weight, logit_scale)


def middle_windows(own, mine, beside, qkv_weight, out_weight, queries):
    return pl.pallas_call(
        middle_kernel,
        out_shape=(
            jax.ShapeDtypeStruct((6, COLS, Z, D), jnp.float32),
            jax.ShapeDtypeStruct((288, D), jnp.float32),
            jax.ShapeDtypeStruct((288, D), jnp.float32),
            jax.ShapeDtypeStruct((D, D), jnp.bfloat16),
        ),
        in_specs=[VMEM] * 7 + [HBM, VMEM],
        out_specs=(VMEM,) * 4,
        scratch_shapes=[pltpu.VMEM((144, D), jnp.bfloat16), pltpu.SemaphoreType.DMA(())],
        compiler_params=pltpu.CompilerParams(vmem_limit_bytes=32 * MIB),
        cost_estimate=pl.CostEstimate(flops=2 << 30, bytes_accessed=2 * MIB, transcendentals=350000),
        name="middle",
    )(
        *own,
        *mine,
        *beside,
        qkv_weight,
        pltpu.with_memory_space_constraint(out_weight, pltpu.HBM),
        queries,
    )


def edge_windows(own, over, qkv_weight, begun, keys, values, queries, out_weight):
    return pl.pallas_call(
        edge_kernel,
        out_shape=jax.ShapeDtypeStruct((ROWS, COLS, Z, D), jnp.float32),
        in_specs=[VMEM] * 11,
        out_specs=HBM,
        scratch_shapes=[
            pltpu.VMEM((2, EDGE, COLS, Z, D), jnp.float32),
            pltpu.VMEM((160, D), jnp.float32),
            pltpu.SemaphoreType.DMA((3,)),
        ],
        compiler_params=pltpu.CompilerParams(vmem_limit_bytes=32 * MIB),
        cost_estimate=pl.CostEstimate(flops=1 << 30, bytes_accessed=2 * MIB, transcendentals=350000),
        name="edges",
    )(*own, *over, qkv_weight, out_weight, keys, values, queries, begun)


def seam_of(axis):
    return lax.axis_size(axis) // 2 - 1


def swapped(value, axis, turn, ring, places=None):
    count = lax.axis_size(axis)
    pairs = []
    for source in range(count) if places is None else places:
        target = source + 1 if source % 2 == turn else source - 1
        if not ring and not 0 <= target < count:
            target = source
        pairs.append((source, target % count))
    return lax.ppermute(value, axis, pairs)


def per_device(
    coarse,
    skip_tokens,
    land_sea,
    surf_table,
    expand_weight,
    expand_gain,
    attn_gain,
    qkv_weight,
    logit_scale,
    out_weight,
):
    own, mine, qkv_weight = expand(
        coarse, skip_tokens, land_sea, surf_table, expand_weight, expand_gain, attn_gain, qkv_weight
    )
    queries = own_queries(mine, qkv_weight, logit_scale)
    beside = []
    for turn in (0, 1):
        beside.append(swapped(mine[turn], "lon", turn, True))
    seam = seam_of("lat")
    at_seam = [seam - 1, seam]
    rows = edge_rows(mine, beside)
    over0 = swapped(rows[0], "lat", 0, False, [at for at in range(lax.axis_size("lat")) if at not in at_seam])
    over1 = swapped(rows[1], "lat", 1, False)
    seam0 = swapped(rows[0], "lat", 0, False, at_seam)
    over = (over0, seam0, over1)
    begun, keys, values, out_weight = middle_windows(own, mine, beside, qkv_weight, out_weight, queries)
    mixed = edge_windows(own, over, qkv_weight, begun, keys, values, queries, out_weight)
    return jnp.transpose(mixed, (2, 0, 1, 3))


def solution(mesh):
    in_specs = (
        P(None, "lat", "lon", None),
        P(None, "lat", "lon", None),
        P("lat", "lon"),
        P(),
        P(),
        P(),
        P(),
        P(),
        P(),
        P(),
    )
    out_specs = P(None, "lat", "lon", None)
    return jax.shard_map(
        per_device, mesh=mesh, in_specs=in_specs, out_specs=out_specs, check_vma=False
    )
```
